256 devices in a mesh: row: 16 (over z_lo, x), col: 16 (over z_hi, y, core).
Axes of the slice: x: 4, y: 4, z: 8 (z_hi: 2, z_lo: 4; z = z_hi * 4 + z_lo), core: 2. Of those that a mesh axis runs over, the one named last changes fastest.
Arguments:
- three_centre: bfloat16 [16, 16, 640, 4096], P('row', 'col'), may hold values from -0.3984375 to 0.3984375
- green_occ: bfloat16 [16, 2, 64, 64], P('row'), may hold values from -0.75 to 0.75
- green_vir: bfloat16 [16, 2, 64, 64], P('col'), may hold values from -0.75 to 0.75
- pair_live: int32 [16, 16], P('row', 'col'), may hold values 0 or 1
Outputs:
- chi_diag: float32 [16, 640, 640], P('row', 'col')
- chi_next: float32 [16, 640, 640], P('row', 'col')
The draws below stay inside these ranges and needn't reach their ends.
All inputs are finite; a program needn't handle non-finite values. No bound on the sum of `pair_live` on one device may be relied on, other than what follows from the above.
Results may differ from the reference program's by a relative error of at most 0.013.
Values may be sent and summed in bfloat16 or wider, within the bound.
A program may use at most 128 MiB of HBM per device.

```python
import jax
import jax.numpy as jnp
from jax import lax

TILE = 64
AUX = 640
NOCC = 16
NVIR = 16


def place_ends(drawn, stream_key, smallest, largest):
    index_at = [jax.random.randint(jax.random.fold_in(stream_key, axis), (), 0, length) for axis, length in enumerate(drawn.shape)]
    main_axis = drawn.shape.index(max(drawn.shape))
    neighbour = index_at[:main_axis] + [(index_at[main_axis] + 1) % drawn.shape[main_axis]] + index_at[main_axis + 1:]
    return drawn.at[tuple(index_at)].set(smallest).at[tuple(neighbour)].set(largest)


def shard_levels(stream_key, shape, pieces, smallest, high):
    loudness = 1.0
    for axis_at, shards_of in pieces:
        steps = jax.random.uniform(jax.random.fold_in(jax.random.fold_in(stream_key, 6), axis_at), (shards_of,), jnp.float32, smallest / len(pieces), high / len(pieces))
        loudness = loudness * jnp.repeat(jnp.exp(steps), shape[axis_at] // shards_of).reshape((-1,) + (1,) * (len(shape) - 1 - axis_at))
    return loudness


def gaussian(rng, extent, deviation, bound, pieces=(), kind=jnp.bfloat16):
    entries = deviation * jax.random.normal(rng, extent, jnp.float32)
    if pieces:
        entries = entries * shard_levels(rng, extent, pieces, -0.22, 0.18)
    return jnp.clip(entries, -bound, bound).astype(kind)


def setup_inputs(seed: int = 0) -> dict:
    seeds = jax.random.split(jax.random.key(seed), 5)
    return {
        "three_centre": gaussian(seeds[0], (NOCC, NVIR, AUX, TILE * TILE), 0.05, 0.3984375, ((0, 16), (1, 16))),
        "green_occ": gaussian(seeds[1], (NOCC, 2, TILE, TILE), TILE ** -0.5, 0.75, ((0, 16),)),
        "green_vir": gaussian(seeds[2], (NVIR, 2, TILE, TILE), TILE ** -0.5, 0.75, ((0, 16),)),
        "pair_live": place_ends((jax.random.randint(seeds[3], (NOCC, NVIR), 0, 4) < 3).astype(jnp.int32), jax.random.fold_in(seeds[3], 1), 0, 1),
    }


def reference(three_centre, green_occ, green_vir, pair_live):
    live = pair_live.astype(jnp.bfloat16)[:, :, None, None]
    blocks = (three_centre * live).reshape(NOCC, NVIR, AUX, TILE, TILE)
    gv_self = green_vir[:, 0].astype(jnp.float32)
    gv_left = green_vir[:, 1].astype(jnp.float32)

    def one_row(n):
        upper = jnp.minimum(n + 1, NOCC - 1).astype(jnp.int32)
        flag = (n < NOCC - 1).astype(jnp.float32)
        own = lax.dynamic_index_in_dim(blocks, n, 0, keepdims=False).astype(jnp.float32)
        above = lax.dynamic_index_in_dim(blocks, upper, 0, keepdims=False).astype(jnp.float32)
        go_self = lax.dynamic_index_in_dim(green_occ, n, 0, keepdims=False)[0].astype(jnp.float32)
        go_down = lax.dynamic_index_in_dim(green_occ, upper, 0, keepdims=False)[1].astype(jnp.float32)
        xa = jnp.einsum('cpml,mn->cpnl', own, go_self).astype(jnp.bfloat16)
        xb = (jnp.einsum('cpml,mn->cpnl', above, go_down) * flag).astype(jnp.bfloat16)
        za = jnp.einsum('cpns,cls->cpnl', own, gv_self).astype(jnp.bfloat16)
        zl = jnp.einsum('cpns,cls->cpnl', own, gv_left).astype(jnp.bfloat16)
        zb = jnp.concatenate([zl[1:], jnp.zeros_like(zl[:1])], axis=0)
        xa = xa.reshape(NVIR, AUX, TILE * TILE).astype(jnp.float32)
        xb = xb.reshape(NVIR, AUX, TILE * TILE).astype(jnp.float32)
        za = za.reshape(NVIR, AUX, TILE * TILE).astype(jnp.float32)
        zb = zb.reshape(NVIR, AUX, TILE * TILE).astype(jnp.float32)
        diag = jnp.einsum('cpk,cqk->pq', xa, za) + jnp.einsum('cpk,cqk->pq', xa, zb)
        nxt = jnp.einsum('cpk,cqk->pq', xb, za) + jnp.einsum('cpk,cqk->pq', xb, zb)
        return diag, nxt

    chi_diag, chi_next = lax.map(one_row, jnp.arange(NOCC, dtype=jnp.int32))
    return chi_diag, chi_next
```

```python
import functools

import jax
import jax.numpy as jnp
from jax import lax
from jax.experimental import pallas as pl
from jax.experimental.pallas import tpu as pltpu
from jax.sharding import PartitionSpec as P

MESH = pl.DeviceIdType.MESH
BF, F32 = jnp.bfloat16, jnp.float32
C = 128
W = 256
STEP = 1024


def dot_nt(a, b):
    return lax.dot_general(a, b, (((1,), (1,)), ((), ())), preferred_element_type=F32)


def dot_nn(a, b):
    return lax.dot_general(a, b, (((1,), (0,)), ((), ())), preferred_element_type=F32)


def kernel(
    rows, cols, tile,
    y_hbm, bdo, bdv, outd, outn,
    y, yr, yd, zt, zin, xa, xb, t32, accd, accn, bdor, bdvr, sd, sn, rd, rn,
    loc_sem, yr_s, yr_r, yd_s, yd_r, z_s, z_r, g_s, g_r, d_s, d_r, n_s, n_r,
):
    n = lax.axis_index("row")
    l = lax.axis_index("col")
    aux, width = y_hbm.shape
    nch = aux // C
    own = aux // cols
    even = lax.rem(l, 2) == 0
    odd = lax.rem(l, 2) == 1
    has_up = n < rows - 1
    has_dn = n > 0
    has_right = l < cols - 1
    has_left = l > 0
    nblk = width // W

    barrier = pltpu.get_barrier_semaphore()

    def hello(r, c):
        pl.semaphore_signal(barrier, inc=1, device_id=(r, c), device_id_type=MESH)

    def hello_col(k, _):
        hello(n, lax.rem(l + k, cols))
        return 0

    lax.fori_loop(1, cols, hello_col, 0)

    @pl.when(has_up)
    def _():
        def f(k, _):
            hello(n + 1, 2 * k)
            return 0
        lax.fori_loop(0, cols // 2, f, 0)

    @pl.when(has_dn & even)
    def _():
        def f(k, _):
            hello(n - 1, k)
            return 0
        lax.fori_loop(0, cols, f, 0)

    @pl.when(has_up & odd)
    def _():
        hello(n + 1, l)

    @pl.when(has_dn & odd)
    def _():
        hello(n - 1, l)

    up, dn, par = has_up.astype(jnp.int32), has_dn.astype(jnp.int32), lax.rem(l, 2)
    from_up = up * (cols // 2 + par)
    from_dn = dn * (cols - par * (cols - 1))
    pl.semaphore_wait(barrier, cols - 1 + from_up + from_dn)

    def chunk(ref, i):
        return ref.at[pl.ds(i * C, C), :]

    def remote(src, dst, ss, rs, r, c):
        return pltpu.make_async_remote_copy(
            src_ref=src, dst_ref=dst, send_sem=ss, recv_sem=rs, device_id=(r, c), device_id_type=MESH)

    def to_left(i):
        return remote(chunk(y_hbm, i), chunk(yr, i), yr_s.at[i], yr_r.at[i], n, l - 1)

    def to_down(i):
        return remote(chunk(y_hbm, i), chunk(yd, i), yd_s.at[i], yd_r.at[i], n - 1, l)

    def z_up(i):
        return remote(zt.at[i], zin.at[i], z_s.at[i], z_r.at[i], n + 1, l)

    gv_left = lambda: remote(bdv.at[1], bdvr, g_s.at[0], g_r.at[0], n, l - 1)
    go_down = lambda: remote(bdo.at[1], bdor, g_s.at[1], g_r.at[1], n - 1, l)

    @pl.when(has_left)
    def _():
        gv_left().start()
        for i in range(nch):
            to_left(i).start()

    @pl.when(has_dn & odd)
    def _():
        go_down().start()
        for i in range(nch):
            to_down(i).start()

    def local(i):
        return pltpu.make_async_copy(chunk(y_hbm, i), chunk(y, i), loc_sem.at[i])

    for i in range(nch):
        local(i).start()
    for i in range(nch):
        local(i).wait()

    def spread(g):
        return jnp.concatenate(
            [t32[pl.ds(g * (W // tile) + j, tile, stride=tile), :] for j in range(W // tile)], axis=0)

    def make_z(i, right):
        def one(b, _):
            at = pl.ds(b * W, W)
            z = dot_nt(bdv[0], y[pl.ds(i * C, C), at])
            if right:
                z = z + dot_nt(bdvr[...], yr[pl.ds(i * C, C), at])
            t32[at, :] = z
            return 0
        lax.fori_loop(0, nblk, one, 0)

        def two(g, _):
            zt[i, pl.ds(g * W, W), :] = spread(g).astype(BF)
            return 0
        lax.fori_loop(0, nblk, two, 0)

    def make_x(src, i, targets):
        def one(b, _):
            at = pl.ds(b * W, W)
            t32[at, :] = dot_nt(bdo[2], src[pl.ds(i * C, C), at])
            return 0
        lax.fori_loop(0, nblk, one, 0)

        def two(g, _):
            part = jnp.transpose(spread(g)).astype(BF)
            for green, dst in targets:
                dst[pl.ds(i * C, C), pl.ds(g * W, W)] = dot_nn(part, green()).astype(BF)
            return 0
        lax.fori_loop(0, nblk, two, 0)

    def chi_cols(acc, i, x, z):
        acc[i] = jnp.zeros((aux, C), F32)

        def one(k, _):
            at = pl.ds(k * STEP, STEP)
            acc[i] += dot_nn(x[:, at], z[i, at, :])
            return 0
        lax.fori_loop(0, width // STEP, one, 0)

    def chi_tile(acc, p, q, x, z):
        at_p = pl.ds(p * C, C)
        acc[q, at_p, :] = dot_nn(x[at_p, :], z[q])

    def piece(send, recv, ss, rs, i, r, c):
        return remote(send.at[i, c], recv.at[i, l], ss.at[i, c], rs.at[i, l], r, c)

    def fill(acc, send, i):
        for d in range(cols):
            send[i, d] = acc[i, d * own:(d + 1) * own, :].astype(BF)

    def scatter_d(i):
        fill(accd, sd, i)
        rd[i, l] = sd[i, l]

        def one(k, _):
            piece(sd, rd, d_s, d_r, i, n, lax.rem(l + k, cols)).start()
            return 0
        lax.fori_loop(1, cols, one, 0)

    def scatter_n_even(i):
        fill(accn, sn, i)

        def one(k, _):
            piece(sn, rn, n_s, n_r, i, n - 1, k).start()
            return 0
        lax.fori_loop(0, cols, one, 0)

    def scatter_n_odd(i):
        fill(accn, sn, i)
        rn[i, l] = sn[i, l]

        def one(k, _):
            piece(sn, rn, n_s, n_r, i, n, lax.rem(l + k, cols)).start()
            return 0
        lax.fori_loop(1, cols, one, 0)

    def each(f):
        def g(i, _):
            f(i)
            return 0
        lax.fori_loop(0, nch, g, 0)

    @pl.when(even)
    def _():
        remote(bdv.at[1], bdvr, g_s.at[0], g_r.at[0], n, l).wait_recv()

        def first(i):
            remote(chunk(y_hbm, i), chunk(yr, i), yr_s.at[i], yr_r.at[i], n, l).wait_recv()
            make_z(i, True)

            @pl.when(has_up)
            def _():
                z_up(i).start()
        each(first)
        each(lambda i: make_x(y, i, ((lambda: bdo[0], xa), (lambda: bdo[1], xb))))

        def second(i):
            chi_cols(accd, i, xa, zt)
            scatter_d(i)
        each(second)

        @pl.when(has_dn)
        def _():
            def third(i):
                remote(zt.at[i], zin.at[i], z_s.at[i], z_r.at[i], n, l).wait_recv()
                chi_cols(accn, i, xb, zin)
                scatter_n_even(i)
            each(third)

    @pl.when(odd)
    def _():
        each(lambda i: make_x(y, i, ((lambda: bdo[0], xa),)))

        @pl.when(has_right)
        def _():
            remote(bdv.at[1], bdvr, g_s.at[0], g_r.at[0], n, l).wait_recv()

        @pl.when(has_up)
        def _():
            remote(bdo.at[1], bdor, g_s.at[1], g_r.at[1], n, l).wait_recv()

        def step(i):
            @pl.when(has_right)
            def _():
                remote(chunk(y_hbm, i), chunk(yr, i), yr_s.at[i], yr_r.at[i], n, l).wait_recv()
                make_z(i, True)

            @pl.when(jnp.logical_not(has_right))
            def _():
                make_z(i, False)
            chi_cols(accd, i, xa, zt)
            scatter_d(i)

            @pl.when(has_up)
            def _():
                remote(chunk(y_hbm, i), chunk(yd, i), yd_s.at[i], yd_r.at[i], n, l).wait_recv()
                make_x(yd, i, ((lambda: bdor[...], xb),))

                def a(p, _):
                    chi_tile(accn, p, i, xb, zt)
                    return 0
                lax.fori_loop(0, i + 1, a, 0)

                def b(q, _):
                    chi_tile(accn, i, q, xb, zt)
                    return 0
                lax.fori_loop(0, i, b, 0)
        each(step)

        @pl.when(has_up)
        def _():
            each(scatter_n_odd)

    def add_up(recv, out):
        for i in range(nch):
            total = recv[i, 0].astype(F32)
            for j in range(1, cols):
                total = total + recv[i, j].astype(F32)
            out[:, i * C:(i + 1) * C] = total

    def got_d(i):
        def one(k, _):
            j = lax.rem(l + k, cols)
            remote(sd.at[i, j], rd.at[i, j], d_s.at[i, j], d_r.at[i, j], n, l).wait_recv()
            return 0
        lax.fori_loop(1, cols, one, 0)
    each(got_d)
    add_up(rd, outd)

    @pl.when(has_up)
    def _():
        def got_n(i):
            def one(k, _):
                remote(sn.at[i, k], rn.at[i, k], n_s.at[i, k], n_r.at[i, k], n, l).wait_recv()
                return 0

            @pl.when(even)
            def _():
                lax.fori_loop(0, cols, one, 0)

            @pl.when(odd)
            def _():
                lax.fori_loop(1, cols, lambda k, c: one(lax.rem(l + k, cols), c), 0)
        each(got_n)
        add_up(rn, outn)

    @pl.when(jnp.logical_not(has_up))
    def _():
        outn[...] = jnp.zeros_like(outn)

    @pl.when(has_left)
    def _():
        gv_left().wait_send()
        for i in range(nch):
            to_left(i).wait_send()

    @pl.when(has_dn & odd)
    def _():
        go_down().wait_send()
        for i in range(nch):
            to_down(i).wait_send()

    @pl.when(has_up & even)
    def _():
        for i in range(nch):
            z_up(i).wait_send()

    def sent(send, recv, ss, rs, i, first, r):
        def one(k, _):
            piece(send, recv, ss, rs, i, r, lax.rem(l + k, cols)).wait_send()
            return 0
        lax.fori_loop(first, cols, one, 0)

    each(lambda i: sent(sd, rd, d_s, d_r, i, 1, n))

    @pl.when(has_dn & even)
    def _():
        each(lambda i: sent(sn, rn, n_s, n_r, i, 0, n - 1))

    @pl.when(has_up & odd)
    def _():
        each(lambda i: sent(sn, rn, n_s, n_r, i, 1, n))


def solution(mesh):
    rows, cols = mesh.shape["row"], mesh.shape["col"]

    def body(three_centre, green_occ, green_vir, pair_live):
        aux, width = three_centre.shape[2:]
        tile = green_occ.shape[2]
        nch, own = aux // C, aux // cols
        live = pair_live[0, 0].astype(BF)
        eye = jnp.eye(W // tile, dtype=BF)

        def diagonal(g):
            wide = eye[None, :, None, :, None] * g[:, None, :, None, :]
            return wide.reshape(g.shape[0], W, W)

        bdo = jnp.concatenate([diagonal(green_occ[0] * live), jnp.eye(W, dtype=BF)[None]], axis=0)
        bdv = diagonal(green_vir[0] * live)
        dma = pltpu.SemaphoreType.DMA
        vm = lambda *s: pltpu.VMEM(s, BF)
        outd, outn = pl.pallas_call(
            functools.partial(kernel, rows, cols, tile),
            out_shape=[jax.ShapeDtypeStruct((own, aux), F32)] * 2,
            in_specs=[
                pl.BlockSpec(memory_space=pl.ANY),
                pl.BlockSpec(memory_space=pltpu.VMEM),
                pl.BlockSpec(memory_space=pltpu.VMEM),
            ],
            out_specs=[pl.BlockSpec(memory_space=pltpu.VMEM)] * 2,
            scratch_shapes=[
                vm(aux, width), vm(aux, width), vm(aux, width),
                vm(nch, width, C), vm(nch, width, C),
                vm(aux, width), vm(aux, width),
                pltpu.VMEM((width, C), F32),
                pltpu.VMEM((nch, aux, C), F32), pltpu.VMEM((nch, aux, C), F32),
                vm(W, W), vm(W, W),
                vm(nch, cols, own, C), vm(nch, cols, own, C),
                vm(nch, cols, own, C), vm(nch, cols, own, C),
                dma((nch,)), dma((nch,)), dma((nch,)), dma((nch,)), dma((nch,)), dma((nch,)), dma((nch,)),
                dma((2,)), dma((2,)),
                dma((nch, cols)), dma((nch, cols)), dma((nch, cols)), dma((nch, cols)),
            ],
            compiler_params=pltpu.CompilerParams(
                collective_id=0, has_side_effects=True, vmem_limit_bytes=60 * 1024 * 1024),
        )(three_centre[0, 0], bdo, bdv)
        return outd[None], outn[None]

    return jax.shard_map(
        body,
        mesh=mesh,
        in_specs=(
            P("row", "col", None, None),
            P("row", None, None, None),
            P("col", None, None, None),
            P("row", "col"),
        ),
        out_specs=(P("row", "col", None), P("row", "col", None)),
        check_vma=False,
    )
```

```python
import functools

import jax
import jax.numpy as jnp
from jax import lax
from jax.experimental import pallas as pl
from jax.experimental.pallas import tpu as pltpu
from jax.sharding import PartitionSpec as P

MESH = pl.DeviceIdType.MESH
BF, F32 = jnp.bfloat16, jnp.float32
C = 128
W = 256
STEP = 1024


def dot_nt(a, b):
    return lax.dot_general(a, b, (((1,), (1,)), ((), ())), preferred_element_type=F32)


def dot_nn(a, b):
    return lax.dot_general(a, b, (((1,), (0,)), ((), ())), preferred_element_type=F32)


def kernel(
    rows, cols, tile,
    y_hbm, bdo, bdv, outd, outn,
    y, yr, yd, zt, zin, xa, xb, t32, accd, accn, bdor, bdvr, rel,
    s0d, s0n, r0d, r0n, sad, san, rad, ran, sbd, sbn, rbd, rbn,
    loc_sem, yr_s, yr_r, yd_s, yd_r, z_s, z_r, g_s, g_r, rel_s, rel_r, part_s, part_r,
    d0_s, d0_r, n0_s, n0_r, da_s, da_r, na_s, na_r, db_s, db_r, nb_s, nb_r,
):
    n = lax.axis_index("row")
    l = lax.axis_index("col")
    aux, width = y_hbm.shape
    nch = aux // C
    own = aux // cols
    half = cols // 2
    ny = half // 2
    core = lax.rem(l, 2)
    iy = lax.rem(l // 2, ny)
    iz = l // half
    even = core == 0
    odd = core == 1
    has_up = n < rows - 1
    has_dn = n > 0
    has_right = l < cols - 1
    has_left = l > 0
    nblk = width // W
    wpart = width // ny
    is_src = l == half
    is_dst = l == half - 1
    is_rel = (l > half) & even

    barrier = pltpu.get_barrier_semaphore()

    def hello(cond, r, c):
        @pl.when(cond)
        def _():
            pl.semaphore_signal(barrier, inc=1, device_id=(r, c), device_id_type=MESH)
        return cond.astype(jnp.int32)

    def y_peer(k):
        return iz * half + lax.rem(iy + k, ny) * 2 + core

    z_peer = lax.rem(l + half, cols)
    always = l >= 0
    count = hello(has_left, n, l - 1) + hello(has_right, n, l + 1)
    count += hello(has_up, n + 1, l) + hello(has_dn, n - 1, l)
    count += hello(has_dn & even, n - 1, l + 1) + hello(has_up & odd, n + 1, l - 1)
    count += hello(always, n, z_peer) + hello(is_rel, n, half - 1)
    for k in range(1, ny):
        count += hello(always, n, y_peer(k)) + hello(is_dst, n, half + 2 * k)
    pl.semaphore_wait(barrier, count)

    def chunk(ref, i):
        return ref.at[pl.ds(i * C, C), :]

    def remote(src, dst, ss, rs, r, c):
        return pltpu.make_async_remote_copy(
            src_ref=src, dst_ref=dst, send_sem=ss, recv_sem=rs, device_id=(r, c), device_id_type=MESH)

    def to_left(i):
        return remote(chunk(y_hbm, i), chunk(yr, i), yr_s.at[i], yr_r.at[i], n, l - 1)

    def to_down(i):
        return remote(chunk(y_hbm, i), chunk(yd, i), yd_s.at[i], yd_r.at[i], n - 1, l)

    def z_up(i):
        return remote(zt.at[i], zin.at[i], z_s.at[i], z_r.at[i], n + 1, l)

    gv_left = lambda: remote(bdv.at[1], bdvr, g_s.at[0], g_r.at[0], n, l - 1)
    go_down = lambda: remote(bdo.at[1], bdor, g_s.at[1], g_r.at[1], n - 1, l)

    def cut(ref, i, k):
        return ref.at[pl.ds(i * C, C), pl.ds(k * wpart, wpart)]

    def part_direct(i):
        return remote(cut(y_hbm, i, 0), cut(yr, i, 0), part_s.at[i, 0], part_r.at[i, 0], n, l - 1)

    def part_out(i, k):
        return remote(cut(y_hbm, i, k), rel.at[i], part_s.at[i, k], rel_r.at[i], n, half + 2 * k)

    def part_on(i, k):
        return remote(rel.at[i], cut(yr, i, k), rel_s.at[i], part_r.at[i, k], n, half - 1)

    @pl.when(has_left)
    def _():
        gv_left().start()

    @pl.when(is_src)
    def _():
        for i in range(nch):
            part_direct(i).start()
            for k in range(1, ny):
                part_out(i, k).start()

    @pl.when(has_left & jnp.logical_not(is_src))
    def _():
        for i in range(nch):
            to_left(i).start()

    @pl.when(has_dn & odd)
    def _():
        go_down().start()
        for i in range(nch):
            to_down(i).start()

    def local(i):
        return pltpu.make_async_copy(chunk(y_hbm, i), chunk(y, i), loc_sem.at[i])

    for i in range(nch):
        local(i).start()
    for i in range(nch):
        local(i).wait()

    def spread(g):
        return jnp.concatenate(
            [t32[pl.ds(g * (W // tile) + j, tile, stride=tile), :] for j in range(W // tile)], axis=0)

    def make_z(i, right):
        def one(b, _):
            at = pl.ds(b * W, W)
            z = dot_nt(bdv[0], y[pl.ds(i * C, C), at])
            if right:
                z = z + dot_nt(bdvr[...], yr[pl.ds(i * C, C), at])
            t32[at, :] = z
            return 0
        lax.fori_loop(0, nblk, one, 0, unroll=True)

        def two(g, _):
            zt[i, pl.ds(g * W, W), :] = spread(g).astype(BF)
            return 0
        lax.fori_loop(0, nblk, two, 0, unroll=True)

    def make_x(src, i, targets):
        def one(b, _):
            at = pl.ds(b * W, W)
            t32[at, :] = jnp.transpose(src[pl.ds(i * C, C), at].astype(F32))
            return 0
        lax.fori_loop(0, nblk, one, 0, unroll=True)

        def two(g, _):
            part = jnp.transpose(spread(g)).astype(BF)
            for green, dst in targets:
                dst[pl.ds(i * C, C), pl.ds(g * W, W)] = dot_nn(part, green()).astype(BF)
            return 0
        lax.fori_loop(0, nblk, two, 0, unroll=True)

    def chi_cols(acc, i, x, z):
        acc[i] = jnp.zeros((aux, C), F32)

        def one(k, _):
            at = pl.ds(k * STEP, STEP)
            acc[i] += dot_nn(x[:, at], z[i, at, :])
            return 0
        lax.fori_loop(0, width // STEP, one, 0)

    def chi_tile(acc, p, q, x, z):
        at_p = pl.ds(p * C, C)
        acc[q, at_p, :] = dot_nn(x[at_p, :], z[q])

    def fill(acc, s0, i):
        for d in range(cols):
            s0[i, d % 2, d // 2] = acc[i, d * own:(d + 1) * own, :].astype(BF)

    def d0(i):
        return remote(s0d.at[i, 1 - core], r0d.at[i], d0_s.at[i], d0_r.at[i], n, l + 1 - 2 * core)

    def n0_even(i, c):
        return remote(s0n.at[i, c], r0n.at[i, 0], n0_s.at[i, c], n0_r.at[i, 0], n - 1, l + c)

    def n0_odd(i):
        return remote(s0n.at[i, 0], r0n.at[i, 1], n0_s.at[i, 0], n0_r.at[i, 1], n, l - 1)

    def scatter_d(i):
        fill(accd, s0d, i)
        d0(i).start()

    def scatter_n_even(i):
        fill(accn, s0n, i)
        n0_even(i, 0).start()
        n0_even(i, 1).start()

    def scatter_n_odd(i):
        fill(accn, s0n, i)
        n0_odd(i).start()

    def a_copy(sa, ra, ss, rs, i, k):
        to = lax.rem(iy + k, ny)
        return remote(sa.at[i, to], ra.at[i, iy], ss.at[i, to], rs.at[i, iy], n, y_peer(k))

    def a_send(first, second, sa, ra, ss, rs, i):
        for z in range(2):
            for k in range(ny):
                at = z * ny + k
                sa[i, k, z] = (first(at).astype(F32) + second(at).astype(F32)).astype(BF)
        ra[i, iy] = sa[i, iy]
        for k in range(1, ny):
            a_copy(sa, ra, ss, rs, i, k).start()

    def a_d(i):
        d0(i).wait_recv()
        a_send(lambda at: s0d[i, core, at], lambda at: r0d[i, at], sad, rad, da_s, da_r, i)

    def a_n(i):
        n0_even(i, 0).wait_recv()

        @pl.when(even)
        def _():
            n0_odd(i).wait_recv()
            a_send(lambda at: r0n[i, 0, at], lambda at: r0n[i, 1, at], san, ran, na_s, na_r, i)

        @pl.when(odd)
        def _():
            a_send(lambda at: r0n[i, 0, at], lambda at: s0n[i, 1, at], san, ran, na_s, na_r, i)

    def b_copy(sb, rb, ss, rs, i):
        return remote(sb.at[i], rb.at[i], ss.at[i], rs.at[i], n, z_peer)

    def b_send(sa, ra, sas, sar, sb, rb, ss, rs, out, i):
        for k in range(1, ny):
            j = lax.rem(iy + k, ny)
            remote(sa.at[i, j], ra.at[i, j], sas.at[i, j], sar.at[i, j], n, l).wait_recv()

        def total(z):
            t = ra[i, 0, z].astype(F32)
            for j in range(1, ny):
                t = t + ra[i, j, z].astype(F32)
            return t
        sb[i] = total(1 - iz).astype(BF)
        b_copy(sb, rb, ss, rs, i).start()
        out[:, pl.ds(pl.multiple_of(i * C, C), C)] = total(iz)

    def b_d(i):
        b_send(sad, rad, da_s, da_r, sbd, rbd, db_s, db_r, outd, i)

    def b_n(i):
        b_send(san, ran, na_s, na_r, sbn, rbn, nb_s, nb_r, outn, i)

    def last(sb, rb, ss, rs, out, i):
        b_copy(sb, rb, ss, rs, i).wait_recv()
        out[:, pl.ds(pl.multiple_of(i * C, C), C)] += rb[i].astype(F32)

    def settle(i):
        @pl.when(i >= 1)
        def _():
            a_d(i - 1)

        @pl.when(i >= 2)
        def _():
            b_d(i - 2)

    def each(f):
        def g(i, _):
            f(i)
            return 0
        lax.fori_loop(0, nch, g, 0)

    def right_chunk(i):
        return remote(chunk(y_hbm, i), chunk(yr, i), yr_s.at[i], yr_r.at[i], n, l)

    @pl.when(even)
    def _():
        remote(bdv.at[1], bdvr, g_s.at[0], g_r.at[0], n, l).wait_recv()

        def first(i):
            right_chunk(i).wait_recv()
            make_z(i, True)

            @pl.when(has_up)
            def _():
                z_up(i).start()

            @pl.when(is_rel)
            def _():
                part_out(i, 1).wait_recv()
                part_on(i, iy).start()
        each(first)
        each(lambda i: make_x(y, i, ((lambda: bdo[0], xa), (lambda: bdo[1], xb))))

        def second(i):
            chi_cols(accd, i, xa, zt)
            scatter_d(i)
        each(second)

        def third(i):
            @pl.when(has_dn)
            def _():
                remote(zt.at[i], zin.at[i], z_s.at[i], z_r.at[i], n, l).wait_recv()
                chi_cols(accn, i, xb, zin)
                scatter_n_even(i)
            settle(i)
        each(third)

    @pl.when(odd)
    def _():
        each(lambda i: make_x(y, i, ((lambda: bdo[0], xa),)))

        @pl.when(has_right)
        def _():
            remote(bdv.at[1], bdvr, g_s.at[0], g_r.at[0], n, l).wait_recv()

        @pl.when(has_up)
        def _():
            remote(bdo.at[1], bdor, g_s.at[1], g_r.at[1], n, l).wait_recv()

        def step(i):
            @pl.when(has_right)
            def _():
                @pl.when(is_dst)
                def _():
                    for k in range(ny):
                        remote(cut(y_hbm, i, k), cut(yr, i, k), part_s.at[i, k], part_r.at[i, k], n, l).wait_recv()

                @pl.when(jnp.logical_not(is_dst))
                def _():
                    right_chunk(i).wait_recv()
                make_z(i, True)

            @pl.when(jnp.logical_not(has_right))
            def _():
                make_z(i, False)
            chi_cols(accd, i, xa, zt)
            scatter_d(i)

            @pl.when(has_up)
            def _():
                remote(chunk(y_hbm, i), chunk(yd, i), yd_s.at[i], yd_r.at[i], n, l).wait_recv()
                make_x(yd, i, ((lambda: bdor[...], xb),))

                def a(p, _):
                    chi_tile(accn, p, i, xb, zt)
                    return 0
                lax.fori_loop(0, i + 1, a, 0)

                def b(q, _):
                    chi_tile(accn, i, q, xb, zt)
                    return 0
                lax.fori_loop(0, i, b, 0)
            settle(i)
        each(step)

        @pl.when(has_up)
        def _():
            each(scatter_n_odd)

    a_d(nch - 1)

    @pl.when(has_up)
    def _():
        each(a_n)
    b_d(nch - 2)
    b_d(nch - 1)

    @pl.when(has_up)
    def _():
        each(b_n)
    each(lambda i: last(sbd, rbd, db_s, db_r, outd, i))

    @pl.when(has_up)
    def _():
        each(lambda i: last(sbn, rbn, nb_s, nb_r, outn, i))

    @pl.when(jnp.logical_not(has_up))
    def _():
        outn[...] = jnp.zeros_like(outn)

    @pl.when(has_left)
    def _():
        gv_left().wait_send()

    @pl.when(is_src)
    def _():
        for i in range(nch):
            part_direct(i).wait_send()
            for k in range(1, ny):
                part_out(i, k).wait_send()

    @pl.when(is_rel)
    def _():
        for i in range(nch):
            part_on(i, iy).wait_send()

    @pl.when(has_left & jnp.logical_not(is_src))
    def _():
        for i in range(nch):
            to_left(i).wait_send()

    @pl.when(has_dn & odd)
    def _():
        go_down().wait_send()
        for i in range(nch):
            to_down(i).wait_send()

    @pl.when(has_up & even)
    def _():
        for i in range(nch):
            z_up(i).wait_send()

    def sent_d(i):
        d0(i).wait_send()
        b_copy(sbd, rbd, db_s, db_r, i).wait_send()
        for k in range(1, ny):
            a_copy(sad, rad, da_s, da_r, i, k).wait_send()
    each(sent_d)

    @pl.when(has_up)
    def _():
        def sent_n(i):
            b_copy(sbn, rbn, nb_s, nb_r, i).wait_send()
            for k in range(1, ny):
                a_copy(san, ran, na_s, na_r, i, k).wait_send()
        each(sent_n)

    @pl.when(has_dn & even)
    def _():
        each(lambda i: (n0_even(i, 0).wait_send(), n0_even(i, 1).wait_send()))

    @pl.when(has_up & odd)
    def _():
        each(lambda i: n0_odd(i).wait_send())


def solution(mesh):
    rows, cols = mesh.shape["row"], mesh.shape["col"]

    def body(three_centre, green_occ, green_vir, pair_live):
        aux, width = three_centre.shape[2:]
        tile = green_occ.shape[2]
        nch, own = aux // C, aux // cols
        half = cols // 2
        ny = half // 2
        live = pair_live[0, 0].astype(BF)
        eye = jnp.eye(W // tile, dtype=BF)

        def diagonal(g):
            wide = eye[None, :, None, :, None] * g[:, None, :, None, :]
            return wide.reshape(g.shape[0], W, W)

        bdo = diagonal(green_occ[0] * live)
        bdv = diagonal(green_vir[0] * live)
        dma = pltpu.SemaphoreType.DMA
        vm = lambda *s: pltpu.VMEM(s, BF)
        outd, outn = pl.pallas_call(
            functools.partial(kernel, rows, cols, tile),
            out_shape=[jax.ShapeDtypeStruct((own, aux), F32)] * 2,
            in_specs=[
                pl.BlockSpec(memory_space=pl.ANY),
                pl.BlockSpec(memory_space=pltpu.VMEM),
                pl.BlockSpec(memory_space=pltpu.VMEM),
            ],
            out_specs=[pl.BlockSpec(memory_space=pltpu.VMEM)] * 2,
            scratch_shapes=[
                vm(aux, width), vm(aux, width), vm(aux, width),
                vm(nch, width, C), vm(nch, width, C),
                vm(aux, width), vm(aux, width),
                pltpu.VMEM((width, C), F32),
                pltpu.VMEM((nch, aux, C), F32), pltpu.VMEM((nch, aux, C), F32),
                vm(W, W), vm(W, W), vm(nch, C, width // ny),
                vm(nch, 2, half, own, C), vm(nch, 2, half, own, C), vm(nch, half, own, C), vm(nch, 2, half, own, C),
                vm(nch, ny, 2, own, C), vm(nch, ny, 2, own, C), vm(nch, ny, 2, own, C), vm(nch, ny, 2, own, C),
                vm(nch, own, C), vm(nch, own, C), vm(nch, own, C), vm(nch, own, C),
                *[dma((nch,))] * 7,
                dma((2,)), dma((2,)), dma((nch,)), dma((nch,)), dma((nch, ny)), dma((nch, ny)),
                dma((nch,)), dma((nch,)), dma((nch, 2)), dma((nch, 2)),
                *[dma((nch, ny))] * 4, *[dma((nch,))] * 4,
            ],
            compiler_params=pltpu.CompilerParams(
                collective_id=0, has_side_effects=True, vmem_limit_bytes=60 * 1024 * 1024),
        )(three_centre[0, 0], bdo, bdv)
        return outd[None], outn[None]

    return jax.shard_map(
        body,
        mesh=mesh,
        in_specs=(
            P("row", "col", None, None),
            P("row", None, None, None),
            P("col", None, None, None),
            P("row", "col"),
        ),
        out_specs=(P("row", "col", None), P("row", "col", None)),
        check_vma=False,
    )
```

```python
import functools
import math

import jax
import jax.numpy as jnp
from jax import lax
from jax.experimental import pallas as pl
from jax.experimental.pallas import tpu as pltpu
from jax.sharding import PartitionSpec as P

MESH = pl.DeviceIdType.MESH
BF, F32 = jnp.bfloat16, jnp.float32
C = 128
W = 256
STEP = 1024


def dot_nt(a, b):
    return lax.dot_general(a, b, (((1,), (1,)), ((), ())), preferred_element_type=F32)


def dot_nn(a, b):
    return lax.dot_general(a, b, (((1,), (0,)), ((), ())), preferred_element_type=F32)


def shares(width, ny):
    through = [k for k in range(ny) if k != 1 or ny < 3]
    edges = [width // 128 * j // len(through) * 128 for j in range(len(through) + 1)]
    return {k: (edges[j], edges[j + 1] - edges[j]) for j, k in enumerate(through)}


def kernel(
    rows, cols, nx, tile,
    y_hbm, bdo, bdv, outd, outn,
    y, yr, yd, zt, zin, xa, xb, t32, accd, accn, bdor, bdvr, rel, rely, relz,
    s0d, s0n, r0d, r0n, sad, san, rad, ran, sbd, sbn, rbd, rbn,
    loc_sem, yr_s, yr_r, yd_s, yd_r, z_s, z_r, g_s, g_r, rel_s, rel_r, part_s, part_r,
    ry_s, ry_r, yw_s, yw_r, rz_s, rz_r, zw_s, zw_r,
    d0_s, d0_r, n0_s, n0_r, da_s, da_r, na_s, na_r, db_s, db_r, nb_s, nb_r,
):
    n = lax.axis_index("row")
    l = lax.axis_index("col")
    aux, width = y_hbm.shape
    nch = aux // C
    own = aux // cols
    half = cols // 2
    ny = half // 2
    core = lax.rem(l, 2)
    iy = lax.rem(l // 2, ny)
    iz = l // half
    even = core == 0
    odd = core == 1
    has_up = n < rows - 1
    has_dn = n > 0
    has_right = l < cols - 1
    has_left = l > 0
    nblk = width // W
    parts = shares(width, ny)
    is_src = l == half
    is_dst = l == half - 1
    through = [k for k in parts if k > 0]
    is_rel = l < 0
    for k in through:
        is_rel = is_rel | (l == half + 2 * k)

    lead, tail = lax.rem(n, nx) == 0, lax.rem(n, nx) == nx - 1
    src_y, rel_y, dst_y = odd & lead & has_dn, odd & tail & (n >= nx), odd & tail & has_up
    src_z, rel_z, dst_z = even & tail & has_up, even & lead & (n + nx < rows), even & lead & has_dn

    barrier = pltpu.get_barrier_semaphore()

    def hello(cond, r, c):
        @pl.when(cond)
        def _():
            pl.semaphore_signal(barrier, inc=1, device_id=(r, c), device_id_type=MESH)
        return cond.astype(jnp.int32)

    def y_peer(k):
        return iz * half + lax.rem(iy + k, ny) * 2 + core

    z_peer = lax.rem(l + half, cols)
    always = l >= 0
    count = hello(has_left, n, l - 1) + hello(has_right, n, l + 1)
    count += hello(has_up, n + 1, l) + hello(has_dn, n - 1, l)
    count += hello(has_dn & even, n - 1, l + 1) + hello(has_up & odd, n + 1, l - 1)
    count += hello(always, n, z_peer) + hello(is_rel, n, half - 1)
    count += hello(src_y, n + nx - 1, l) + hello(rel_y, n - nx + 1, l)
    count += hello(rel_y, n - nx, l) + hello(dst_y, n + nx, l)
    count += hello(src_z, n - nx + 1, l) + hello(rel_z, n + nx - 1, l)
    count += hello(rel_z, n + nx, l) + hello(dst_z, n - nx, l)
    for k in range(1, ny):
        count += hello(always, n, y_peer(k))
    for k in through:
        count += hello(is_dst, n, half + 2 * k)
    pl.semaphore_wait(barrier, count)

    def chunk(ref, i):
        return ref.at[pl.ds(i * C, C), :]

    def remote(src, dst, ss, rs, r, c):
        return pltpu.make_async_remote_copy(
            src_ref=src, dst_ref=dst, send_sem=ss, recv_sem=rs, device_id=(r, c), device_id_type=MESH)

    def to_left(i):
        return remote(chunk(y_hbm, i), chunk(yr, i), yr_s.at[i], yr_r.at[i], n, l - 1)

    def to_down(i):
        return remote(chunk(y_hbm, i), chunk(yd, i), yd_s.at[i], yd_r.at[i], n - 1, l)

    def z_up(i):
        return remote(zt.at[i], zin.at[i], z_s.at[i], z_r.at[i], n + 1, l)

    gv_left = lambda: remote(bdv.at[1], bdvr, g_s.at[0], g_r.at[0], n, l - 1)
    go_down = lambda: remote(bdo.at[1], bdor, g_s.at[1], g_r.at[1], n - 1, l)

    def cut(ref, i, k):
        at, size = parts[k]
        return ref.at[pl.ds(i * C, C), pl.ds(at, size)]

    def part_direct(i):
        return remote(cut(y_hbm, i, 0), cut(yr, i, 0), part_s.at[i, 0], part_r.at[i, 0], n, l - 1)

    def part_out(i, k):
        return remote(cut(y_hbm, i, k), rel.at[i, :, pl.ds(0, parts[k][1])], part_s.at[i, k], rel_r.at[i], n, half + 2 * k)

    def part_on(i, k):
        return remote(rel.at[i, :, pl.ds(0, parts[k][1])], cut(yr, i, k), rel_s.at[i], part_r.at[i, k], n, half - 1)

    @pl.when(has_left)
    def _():
        gv_left().start()

    @pl.when(is_src)
    def _():
        for i in range(nch):
            part_direct(i).start()
            for k in through:
                part_out(i, k).start()

    @pl.when(has_left & jnp.logical_not(is_src))
    def _():
        for i in range(nch):
            to_left(i).start()

    def side_y(ref, i, h):
        return ref.at[pl.ds(i * C, C), pl.ds(h * (width // 2), width // 2)]

    def side_z(ref, i, h):
        return ref.at[i, pl.ds(h * (width // 2), width // 2), :]

    def yw_direct(i):
        return remote(side_y(y_hbm, i, 0), side_y(yd, i, 0), yw_s.at[i, 0], yw_r.at[i, 0], n - 1, l)

    def yw_out(i):
        return remote(side_y(y_hbm, i, 1), rely.at[i], yw_s.at[i, 1], ry_r.at[i], n + nx - 1, l)

    def yw_on(i):
        return remote(rely.at[i], side_y(yd, i, 1), ry_s.at[i], yw_r.at[i, 1], n - nx, l)

    def zw_direct(i):
        return remote(side_z(zt, i, 0), side_z(zin, i, 0), zw_s.at[i, 0], zw_r.at[i, 0], n + 1, l)

    def zw_out(i):
        return remote(side_z(zt, i, 1), relz.at[i], zw_s.at[i, 1], rz_r.at[i], n - nx + 1, l)

    def zw_on(i):
        return remote(relz.at[i], side_z(zin, i, 1), rz_s.at[i], zw_r.at[i, 1], n + nx, l)

    plain_y = has_dn & odd & jnp.logical_not(lead)
    plain_z = has_up & even & jnp.logical_not(tail)

    @pl.when(has_dn & odd)
    def _():
        go_down().start()

    @pl.when(src_y)
    def _():
        for i in range(nch):
            yw_direct(i).start()
            yw_out(i).start()

    @pl.when(plain_y)
    def _():
        for i in range(nch):
            to_down(i).start()

    def local(i):
        return pltpu.make_async_copy(chunk(y_hbm, i), chunk(y, i), loc_sem.at[i])

    for i in range(nch):
        local(i).start()
    for i in range(nch):
        local(i).wait()

    def spread(g):
        return jnp.concatenate(
            [t32[pl.ds(g * (W // tile) + j, tile, stride=tile), :] for j in range(W // tile)], axis=0)

    def make_z(i, right):
        def one(b, _):
            at = pl.ds(b * W, W)
            z = dot_nt(bdv[0], y[pl.ds(i * C, C), at])
            if right:
                z = z + dot_nt(bdvr[...], yr[pl.ds(i * C, C), at])
            t32[at, :] = z
            return 0
        lax.fori_loop(0, nblk, one, 0, unroll=True)

        def two(g, _):
            zt[i, pl.ds(g * W, W), :] = spread(g).astype(BF)
            return 0
        lax.fori_loop(0, nblk, two, 0, unroll=True)

    def make_x(src, i, targets):
        def one(b, _):
            at = pl.ds(b * W, W)
            t32[at, :] = jnp.transpose(src[pl.ds(i * C, C), at].astype(F32))
            return 0
        lax.fori_loop(0, nblk, one, 0, unroll=True)

        def two(g, _):
            part = jnp.transpose(spread(g)).astype(BF)
            for green, dst in targets:
                dst[pl.ds(i * C, C), pl.ds(g * W, W)] = dot_nn(part, green()).astype(BF)
            return 0
        lax.fori_loop(0, nblk, two, 0, unroll=True)

    def chi_cols(acc, i, x, z):
        acc[i] = jnp.zeros((aux, C), F32)

        def one(k, _):
            at = pl.ds(k * STEP, STEP)
            acc[i] += dot_nn(x[:, at], z[i, at, :])
            return 0
        lax.fori_loop(0, width // STEP, one, 0)

    def chi_tile(acc, p, q, x, z):
        at_p = pl.ds(p * C, C)
        acc[q, at_p, :] = dot_nn(x[at_p, :], z[q])

    def fill(acc, s0, i):
        for d in range(cols):
            s0[i, d % 2, d // 2] = acc[i, d * own:(d + 1) * own, :].astype(BF)

    def d0(i):
        return remote(s0d.at[i, 1 - core], r0d.at[i], d0_s.at[i], d0_r.at[i], n, l + 1 - 2 * core)

    def n0_even(i, c):
        return remote(s0n.at[i, c], r0n.at[i, 0], n0_s.at[i, c], n0_r.at[i, 0], n - 1, l + c)

    def n0_odd(i):
        return remote(s0n.at[i, 0], r0n.at[i, 1], n0_s.at[i, 0], n0_r.at[i, 1], n, l - 1)

    def scatter_d(i):
        fill(accd, s0d, i)
        d0(i).start()

    def scatter_n_even(i):
        fill(accn, s0n, i)
        n0_even(i, 0).start()
        n0_even(i, 1).start()

    def scatter_n_odd(i):
        fill(accn, s0n, i)
        n0_odd(i).start()

    def a_copy(sa, ra, ss, rs, i, k):
        to = lax.rem(iy + k, ny)
        return remote(sa.at[i, to], ra.at[i, iy], ss.at[i, to], rs.at[i, iy], n, y_peer(k))

    def a_send(first, second, sa, ra, ss, rs, i):
        for z in range(2):
            for k in range(ny):
                at = z * ny + k
                sa[i, k, z] = (first(at).astype(F32) + second(at).astype(F32)).astype(BF)
        ra[i, iy] = sa[i, iy]
        for k in range(1, ny):
            a_copy(sa, ra, ss, rs, i, k).start()

    def a_d(i):
        d0(i).wait_recv()
        a_send(lambda at: s0d[i, core, at], lambda at: r0d[i, at], sad, rad, da_s, da_r, i)

    def a_n(i):
        n0_even(i, 0).wait_recv()

        @pl.when(even)
        def _():
            n0_odd(i).wait_recv()
            a_send(lambda at: r0n[i, 0, at], lambda at: r0n[i, 1, at], san, ran, na_s, na_r, i)

        @pl.when(odd)
        def _():
            a_send(lambda at: r0n[i, 0, at], lambda at: s0n[i, 1, at], san, ran, na_s, na_r, i)

    def b_copy(sb, rb, ss, rs, i):
        return remote(sb.at[i], rb.at[i], ss.at[i], rs.at[i], n, z_peer)

    def b_send(sa, ra, sas, sar, sb, rb, ss, rs, out, i):
        for k in range(1, ny):
            j = lax.rem(iy + k, ny)
            remote(sa.at[i, j], ra.at[i, j], sas.at[i, j], sar.at[i, j], n, l).wait_recv()

        def total(z):
            t = ra[i, 0, z].astype(F32)
            for j in range(1, ny):
                t = t + ra[i, j, z].astype(F32)
            return t
        sb[i] = total(1 - iz).astype(BF)
        b_copy(sb, rb, ss, rs, i).start()
        out[:, pl.ds(pl.multiple_of(i * C, C), C)] = total(iz)

    def b_d(i):
        b_send(sad, rad, da_s, da_r, sbd, rbd, db_s, db_r, outd, i)

    def b_n(i):
        b_send(san, ran, na_s, na_r, sbn, rbn, nb_s, nb_r, outn, i)

    def last(sb, rb, ss, rs, out, i):
        b_copy(sb, rb, ss, rs, i).wait_recv()
        out[:, pl.ds(pl.multiple_of(i * C, C), C)] += rb[i].astype(F32)

    def settle(i):
        @pl.when(i >= 1)
        def _():
            a_d(i - 1)

    def each(f):
        def g(i, _):
            f(i)
            return 0
        lax.fori_loop(0, nch, g, 0)

    def right_chunk(i):
        return remote(chunk(y_hbm, i), chunk(yr, i), yr_s.at[i], yr_r.at[i], n, l)

    @pl.when(even)
    def _():
        remote(bdv.at[1], bdvr, g_s.at[0], g_r.at[0], n, l).wait_recv()

        def first(i):
            right_chunk(i).wait_recv()
            make_z(i, True)

            @pl.when(plain_z)
            def _():
                z_up(i).start()

            @pl.when(src_z)
            def _():
                zw_direct(i).start()
                zw_out(i).start()

            for k in through:
                @pl.when(l == half + 2 * k)
                def _():
                    part_out(i, k).wait_recv()
                    part_on(i, k).start()
        each(first)
        each(lambda i: make_x(y, i, ((lambda: bdo[0], xa), (lambda: bdo[1], xb))))

        def pass_z(i):
            @pl.when(rel_z)
            def _():
                zw_out(i).wait_recv()
                zw_on(i).start()
        pass_z(0)

        def second(i):
            chi_cols(accd, i, xa, zt)
            scatter_d(i)
        each(second)

        def third(i):
            @pl.when(has_dn)
            def _():
                @pl.when(lead)
                def _():
                    zw_direct(i).wait_recv()
                    zw_on(i).wait_recv()

                @pl.when(jnp.logical_not(lead))
                def _():
                    remote(zt.at[i], zin.at[i], z_s.at[i], z_r.at[i], n, l).wait_recv()
                chi_cols(accn, i, xb, zin)
                scatter_n_even(i)
            settle(i)

            @pl.when(i < nch - 1)
            def _():
                pass_z(i + 1)
        each(third)

    @pl.when(odd)
    def _():
        each(lambda i: make_x(y, i, ((lambda: bdo[0], xa),)))

        @pl.when(has_right)
        def _():
            remote(bdv.at[1], bdvr, g_s.at[0], g_r.at[0], n, l).wait_recv()

        @pl.when(has_up)
        def _():
            remote(bdo.at[1], bdor, g_s.at[1], g_r.at[1], n, l).wait_recv()

        def step(i):
            @pl.when(rel_y)
            def _():
                yw_out(i).wait_recv()
                yw_on(i).start()

            @pl.when(has_right)
            def _():
                @pl.when(is_dst)
                def _():
                    for k in parts:
                        remote(cut(y_hbm, i, k), cut(yr, i, k), part_s.at[i, k], part_r.at[i, k], n, l).wait_recv()

                @pl.when(jnp.logical_not(is_dst))
                def _():
                    right_chunk(i).wait_recv()
                make_z(i, True)

            @pl.when(jnp.logical_not(has_right))
            def _():
                make_z(i, False)
            chi_cols(accd, i, xa, zt)
            scatter_d(i)

            @pl.when(has_up)
            def _():
                @pl.when(tail)
                def _():
                    yw_direct(i).wait_recv()
                    yw_on(i).wait_recv()

                @pl.when(jnp.logical_not(tail))
                def _():
                    remote(chunk(y_hbm, i), chunk(yd, i), yd_s.at[i], yd_r.at[i], n, l).wait_recv()
                make_x(yd, i, ((lambda: bdor[...], xb),))

                def a(p, _):
                    chi_tile(accn, p, i, xb, zt)
                    return 0
                lax.fori_loop(0, i + 1, a, 0)

                def b(q, _):
                    chi_tile(accn, i, q, xb, zt)
                    return 0
                lax.fori_loop(0, i, b, 0)
            settle(i)
        each(step)

        @pl.when(has_up)
        def _():
            each(scatter_n_odd)

    a_d(nch - 1)

    @pl.when(has_up)
    def _():
        each(a_n)
    each(b_d)

    @pl.when(has_up)
    def _():
        each(b_n)
    each(lambda i: last(sbd, rbd, db_s, db_r, outd, i))

    @pl.when(has_up)
    def _():
        each(lambda i: last(sbn, rbn, nb_s, nb_r, outn, i))

    @pl.when(jnp.logical_not(has_up))
    def _():
        outn[...] = jnp.zeros_like(outn)

    @pl.when(has_left)
    def _():
        gv_left().wait_send()

    @pl.when(is_src)
    def _():
        for i in range(nch):
            part_direct(i).wait_send()
            for k in through:
                part_out(i, k).wait_send()

    for k in through:
        @pl.when(l == half + 2 * k)
        def _():
            for i in range(nch):
                part_on(i, k).wait_send()

    @pl.when(has_left & jnp.logical_not(is_src))
    def _():
        for i in range(nch):
            to_left(i).wait_send()

    @pl.when(has_dn & odd)
    def _():
        go_down().wait_send()

    @pl.when(plain_y)
    def _():
        for i in range(nch):
            to_down(i).wait_send()

    @pl.when(plain_z)
    def _():
        for i in range(nch):
            z_up(i).wait_send()

    @pl.when(src_y)
    def _():
        for i in range(nch):
            yw_direct(i).wait_send()
            yw_out(i).wait_send()

    @pl.when(src_z)
    def _():
        for i in range(nch):
            zw_direct(i).wait_send()
            zw_out(i).wait_send()

    @pl.when(rel_y)
    def _():
        for i in range(nch):
            yw_on(i).wait_send()

    @pl.when(rel_z)
    def _():
        for i in range(nch):
            zw_on(i).wait_send()

    def sent_d(i):
        d0(i).wait_send()
        b_copy(sbd, rbd, db_s, db_r, i).wait_send()
        for k in range(1, ny):
            a_copy(sad, rad, da_s, da_r, i, k).wait_send()
    each(sent_d)

    @pl.when(has_up)
    def _():
        def sent_n(i):
            b_copy(sbn, rbn, nb_s, nb_r, i).wait_send()
            for k in range(1, ny):
                a_copy(san, ran, na_s, na_r, i, k).wait_send()
        each(sent_n)

    @pl.when(has_dn & even)
    def _():
        each(lambda i: (n0_even(i, 0).wait_send(), n0_even(i, 1).wait_send()))

    @pl.when(has_up & odd)
    def _():
        each(lambda i: n0_odd(i).wait_send())


def solution(mesh):
    rows, cols = mesh.shape["row"], mesh.shape["col"]

    def body(three_centre, green_occ, green_vir, pair_live):
        aux, width = three_centre.shape[2:]
        tile = green_occ.shape[2]
        nch, own = aux // C, aux // cols
        half = cols // 2
        ny = half // 2
        nx = math.isqrt(rows)
        live = pair_live[0, 0].astype(BF)
        eye = jnp.eye(W // tile, dtype=BF)

        def diagonal(g):
            wide = eye[None, :, None, :, None] * g[:, None, :, None, :]
            return wide.reshape(g.shape[0], W, W)

        bdo = diagonal(green_occ[0] * live)
        bdv = diagonal(green_vir[0] * live)
        dma = pltpu.SemaphoreType.DMA
        vm = lambda *s: pltpu.VMEM(s, BF)
        outd, outn = pl.pallas_call(
            functools.partial(kernel, rows, cols, nx, tile),
            out_shape=[jax.ShapeDtypeStruct((own, aux), F32)] * 2,
            in_specs=[
                pl.BlockSpec(memory_space=pl.ANY),
                pl.BlockSpec(memory_space=pltpu.VMEM),
                pl.BlockSpec(memory_space=pltpu.VMEM),
            ],
            out_specs=[pl.BlockSpec(memory_space=pltpu.VMEM)] * 2,
            scratch_shapes=[
                vm(aux, width), vm(aux, width), vm(aux, width),
                vm(nch, width, C), vm(nch, width, C),
                vm(aux, width), vm(aux, width),
                pltpu.VMEM((width, C), F32),
                pltpu.VMEM((nch, aux, C), F32), pltpu.VMEM((nch, aux, C), F32),
                vm(W, W), vm(W, W), vm(nch, C, max(size for _, size in shares(width, ny).values())), vm(nch, C, width // 2), vm(nch, width // 2, C),
                vm(nch, 2, half, own, C), vm(nch, 2, half, own, C), vm(nch, half, own, C), vm(nch, 2, half, own, C),
                vm(nch, ny, 2, own, C), vm(nch, ny, 2, own, C), vm(nch, ny, 2, own, C), vm(nch, ny, 2, own, C),
                vm(nch, own, C), vm(nch, own, C), vm(nch, own, C), vm(nch, own, C),
                *[dma((nch,))] * 7,
                dma((2,)), dma((2,)), dma((nch,)), dma((nch,)), dma((nch, ny)), dma((nch, ny)),
                dma((nch,)), dma((nch,)), dma((nch, 2)), dma((nch, 2)), dma((nch,)), dma((nch,)), dma((nch, 2)), dma((nch, 2)),
                dma((nch,)), dma((nch,)), dma((nch, 2)), dma((nch, 2)),
                *[dma((nch, ny))] * 4, *[dma((nch,))] * 4,
            ],
            compiler_params=pltpu.CompilerParams(
                collective_id=0, has_side_effects=True, vmem_limit_bytes=60 * 1024 * 1024),
        )(three_centre[0, 0], bdo, bdv)
        return outd[None], outn[None]

    return jax.shard_map(
        body,
        mesh=mesh,
        in_specs=(
            P("row", "col", None, None),
            P("row", None, None, None),
            P("col", None, None, None),
            P("row", "col"),
        ),
        out_specs=(P("row", "col", None), P("row", "col", None)),
        check_vma=False,
    )
```

```python
import functools
import math

import jax
import jax.numpy as jnp
from jax import lax
from jax.experimental import pallas as pl
from jax.experimental.pallas import tpu as pltpu
from jax.sharding import PartitionSpec as P

MESH = pl.DeviceIdType.MESH
BF, F32 = jnp.bfloat16, jnp.float32
C = 128
W = 256
STEP = 1024


def dot_nt(a, b):
    return lax.dot_general(a, b, (((1,), (1,)), ((), ())), preferred_element_type=F32)


def dot_nn(a, b):
    return lax.dot_general(a, b, (((1,), (0,)), ((), ())), preferred_element_type=F32)


def shares(width, ny):
    weight = [1 if k == 1 and ny > 2 else 3 for k in range(ny)]
    edges = [width // 128 * sum(weight[:k]) // sum(weight) * 128 for k in range(ny + 1)]
    return {k: (edges[k], edges[k + 1] - edges[k]) for k in range(ny)}


def kernel(
    rows, cols, nx, tile,
    y_hbm, green_o, green_v, live, out2,
    bdo, bdv, y, yr, yd, zt, zin, xa, xb, t32, accd, accn, bdor, bdvr, rel, rely, relz,
    s0d, s0n, r0d, r0n, sad, san, rad, ran, sbd, sbn, rbd, rbn,
    loc_sem, yr_s, yr_r, yd_s, yd_r, z_s, z_r, g_s, g_r, rel_s, rel_r, part_s, part_r,
    ry_s, ry_r, yw_s, yw_r, rz_s, rz_r, zw_s, zw_r,
    d0_s, d0_r, n0_s, n0_r, da_s, da_r, na_s, na_r, db_s, db_r, nb_s, nb_r,
):
    n = lax.axis_index("row")
    l = lax.axis_index("col")
    aux, width = y_hbm.shape
    outd, outn = out2.at[0], out2.at[1]
    nch = aux // C
    own = aux // cols
    half = cols // 2
    ny = half // 2
    core = lax.rem(l, 2)
    iy = lax.rem(l // 2, ny)
    iz = l // half
    even = core == 0
    odd = core == 1
    has_up = n < rows - 1
    has_dn = n > 0
    has_right = l < cols - 1
    has_left = l > 0
    nblk = width // W
    parts = shares(width, ny)
    is_src = l == half
    is_dst = l == half - 1
    through = [k for k in parts if k > 0]
    is_rel = l < 0
    for k in through:
        is_rel = is_rel | (l == half + 2 * k)

    lead, tail = lax.rem(n, nx) == 0, lax.rem(n, nx) == nx - 1
    src_y, rel_y, dst_y = odd & lead & has_dn, odd & tail & (n >= nx), odd & tail & has_up
    src_z, rel_z, dst_z = even & tail & has_up, even & lead & (n + nx < rows), even & lead & has_dn

    barrier = pltpu.get_barrier_semaphore()

    def hello(cond, r, c):
        @pl.when(cond)
        def _():
            pl.semaphore_signal(barrier, inc=1, device_id=(r, c), device_id_type=MESH)
        return cond.astype(jnp.int32)

    def y_peer(k):
        return iz * half + lax.rem(iy + k, ny) * 2 + core

    z_peer = lax.rem(l + half, cols)
    always = l >= 0
    count = hello(has_left, n, l - 1) + hello(has_right, n, l + 1)
    count += hello(has_up, n + 1, l) + hello(has_dn, n - 1, l)
    count += hello(has_dn & even, n - 1, l + 1) + hello(has_up & odd, n + 1, l - 1)
    count += hello(always, n, z_peer) + hello(is_rel, n, half - 1)
    count += hello(src_y, n + nx - 1, l) + hello(rel_y, n - nx + 1, l)
    count += hello(rel_y, n - nx, l) + hello(dst_y, n + nx, l)
    count += hello(src_z, n - nx + 1, l) + hello(rel_z, n + nx - 1, l)
    count += hello(rel_z, n + nx, l) + hello(dst_z, n - nx, l)
    for k in range(1, ny):
        count += hello(always, n, y_peer(k))
    for k in through:
        count += hello(is_dst, n, half + 2 * k)
    on = live[0, 0].astype(F32)
    spot = [lax.shift_right_logical(lax.broadcasted_iota(jnp.int32, (W, W), k), tile.bit_length() - 1) for k in range(2)]
    for green, wide in ((green_o, bdo), (green_v, bdv)):
        for k in range(2):
            g = green[k].astype(F32) * on
            g = jnp.concatenate([g] * (W // tile), axis=1)
            g = jnp.concatenate([g] * (W // tile), axis=0)
            wide[k] = jnp.where(spot[0] == spot[1], g, 0.0).astype(BF)
    pl.semaphore_wait(barrier, count)

    def chunk(ref, i):
        return ref.at[pl.ds(i * C, C), :]

    def remote(src, dst, ss, rs, r, c):
        return pltpu.make_async_remote_copy(
            src_ref=src, dst_ref=dst, send_sem=ss, recv_sem=rs, device_id=(r, c), device_id_type=MESH)

    def to_left(i):
        return remote(chunk(y_hbm, i), chunk(yr, i), yr_s.at[i], yr_r.at[i], n, l - 1)

    def to_down(i):
        return remote(chunk(y_hbm, i), chunk(yd, i), yd_s.at[i], yd_r.at[i], n - 1, l)

    def z_up(i):
        return remote(zt.at[i], zin.at[i], z_s.at[i], z_r.at[i], n + 1, l)

    gv_left = lambda: remote(bdv.at[1], bdvr, g_s.at[0], g_r.at[0], n, l - 1)
    go_down = lambda: remote(bdo.at[1], bdor, g_s.at[1], g_r.at[1], n - 1, l)

    def cut(ref, i, k):
        at, size = parts[k]
        return ref.at[pl.ds(i * C, C), pl.ds(at, size)]

    def part_direct(i):
        return remote(cut(y_hbm, i, 0), cut(yr, i, 0), part_s.at[i, 0], part_r.at[i, 0], n, l - 1)

    def part_out(i, k):
        return remote(cut(y_hbm, i, k), rel.at[i, :, pl.ds(0, parts[k][1])], part_s.at[i, k], rel_r.at[i], n, half + 2 * k)

    def part_on(i, k):
        return remote(rel.at[i, :, pl.ds(0, parts[k][1])], cut(yr, i, k), rel_s.at[i], part_r.at[i, k], n, half - 1)

    @pl.when(has_left)
    def _():
        gv_left().start()

    @pl.when(is_src)
    def _():
        for i in range(nch):
            part_direct(i).start()
            for k in through:
                part_out(i, k).start()

    @pl.when(has_left & jnp.logical_not(is_src))
    def _():
        for i in range(nch):
            to_left(i).start()

    def side_y(ref, i, h):
        return ref.at[pl.ds(i * C, C), pl.ds(h * (width // 2), width // 2)]

    def side_z(ref, i, h):
        return ref.at[i, pl.ds(h * (width // 2), width // 2), :]

    def yw_direct(i):
        return remote(side_y(y_hbm, i, 0), side_y(yd, i, 0), yw_s.at[i, 0], yw_r.at[i, 0], n - 1, l)

    def yw_out(i):
        return remote(side_y(y_hbm, i, 1), rely.at[i], yw_s.at[i, 1], ry_r.at[i], n + nx - 1, l)

    def yw_on(i):
        return remote(rely.at[i], side_y(yd, i, 1), ry_s.at[i], yw_r.at[i, 1], n - nx, l)

    def zw_direct(i):
        return remote(side_z(zt, i, 0), side_z(zin, i, 0), zw_s.at[i, 0], zw_r.at[i, 0], n + 1, l)

    def zw_out(i):
        return remote(side_z(zt, i, 1), relz.at[i], zw_s.at[i, 1], rz_r.at[i], n - nx + 1, l)

    def zw_on(i):
        return remote(relz.at[i], side_z(zin, i, 1), rz_s.at[i], zw_r.at[i, 1], n + nx, l)

    plain_y = has_dn & odd & jnp.logical_not(lead)
    plain_z = has_up & even & jnp.logical_not(tail)

    @pl.when(has_dn & odd)
    def _():
        go_down().start()

    @pl.when(src_y)
    def _():
        for i in range(nch):
            yw_direct(i).start()
            yw_out(i).start()

    @pl.when(plain_y)
    def _():
        for i in range(nch):
            to_down(i).start()

    def local(i):
        return pltpu.make_async_copy(chunk(y_hbm, i), chunk(y, i), loc_sem.at[i])

    for i in range(nch):
        local(i).start()
    for i in range(nch):
        local(i).wait()

    def spread(g):
        return jnp.concatenate(
            [t32[pl.ds(g * (W // tile) + j, tile, stride=tile), :] for j in range(W // tile)], axis=0)

    def make_z(i, right):
        def one(b, _):
            at = pl.ds(b * W, W)
            z = dot_nt(bdv[0], y[pl.ds(i * C, C), at])
            if right:
                z = z + dot_nt(bdvr[...], yr[pl.ds(i * C, C), at])
            t32[at, :] = z
            return 0
        lax.fori_loop(0, nblk, one, 0, unroll=True)

        def two(g, _):
            zt[i, pl.ds(g * W, W), :] = spread(g).astype(BF)
            return 0
        lax.fori_loop(0, nblk, two, 0, unroll=True)

    def make_x(src, i, targets):
        def one(b, _):
            at = pl.ds(b * W, W)
            t32[at, :] = jnp.transpose(src[pl.ds(i * C, C), at].astype(F32))
            return 0
        lax.fori_loop(0, nblk, one, 0, unroll=True)

        def two(g, _):
            part = jnp.transpose(spread(g)).astype(BF)
            for green, dst in targets:
                dst[pl.ds(i * C, C), pl.ds(g * W, W)] = dot_nn(part, green()).astype(BF)
            return 0
        lax.fori_loop(0, nblk, two, 0, unroll=True)

    def chi_cols(acc, i, x, z):
        acc[i] = jnp.zeros((aux, C), F32)

        def one(k, _):
            at = pl.ds(k * STEP, STEP)
            acc[i] += dot_nn(x[:, at], z[i, at, :])
            return 0
        lax.fori_loop(0, width // STEP, one, 0)

    def chi_tile(acc, p, q, x, z):
        at_p = pl.ds(p * C, C)
        acc[q, at_p, :] = dot_nn(x[at_p, :], z[q])

    def fill(acc, s0, i):
        for d in range(cols):
            s0[i, d % 2, d // 2] = acc[i, d * own:(d + 1) * own, :].astype(BF)

    def d0(i):
        return remote(s0d.at[i, 1 - core], r0d.at[i], d0_s.at[i], d0_r.at[i], n, l + 1 - 2 * core)

    def n0_even(i, c):
        return remote(s0n.at[i, c], r0n.at[i, 0], n0_s.at[i, c], n0_r.at[i, 0], n - 1, l + c)

    def n0_odd(i):
        return remote(s0n.at[i, 0], r0n.at[i, 1], n0_s.at[i, 0], n0_r.at[i, 1], n, l - 1)

    def scatter_d(i):
        fill(accd, s0d, i)
        d0(i).start()

    def scatter_n_even(i):
        fill(accn, s0n, i)
        n0_even(i, 0).start()
        n0_even(i, 1).start()

    def scatter_n_odd(i):
        fill(accn, s0n, i)
        n0_odd(i).start()

    def a_copy(sa, ra, ss, rs, i, k):
        to = lax.rem(iy + k, ny)
        return remote(sa.at[i, to], ra.at[i, iy], ss.at[i, to], rs.at[i, iy], n, y_peer(k))

    def a_send(first, second, sa, ra, ss, rs, i):
        for z in range(2):
            for k in range(ny):
                at = z * ny + k
                sa[i, k, z] = (first(at).astype(F32) + second(at).astype(F32)).astype(BF)
        ra[i, iy] = sa[i, iy]
        for k in range(1, ny):
            a_copy(sa, ra, ss, rs, i, k).start()

    def a_d(i):
        d0(i).wait_recv()
        a_send(lambda at: s0d[i, core, at], lambda at: r0d[i, at], sad, rad, da_s, da_r, i)

    def a_n(i):
        n0_even(i, 0).wait_recv()

        @pl.when(even)
        def _():
            n0_odd(i).wait_recv()
            a_send(lambda at: r0n[i, 0, at], lambda at: r0n[i, 1, at], san, ran, na_s, na_r, i)

        @pl.when(odd)
        def _():
            a_send(lambda at: r0n[i, 0, at], lambda at: s0n[i, 1, at], san, ran, na_s, na_r, i)

    def b_copy(sb, rb, ss, rs, i):
        return remote(sb.at[i], rb.at[i], ss.at[i], rs.at[i], n, z_peer)

    def b_send(sa, ra, sas, sar, sb, rb, ss, rs, out, i):
        for k in range(1, ny):
            j = lax.rem(iy + k, ny)
            remote(sa.at[i, j], ra.at[i, j], sas.at[i, j], sar.at[i, j], n, l).wait_recv()

        def total(z):
            t = ra[i, 0, z].astype(F32)
            for j in range(1, ny):
                t = t + ra[i, j, z].astype(F32)
            return t
        sb[i] = total(1 - iz).astype(BF)
        b_copy(sb, rb, ss, rs, i).start()
        out[:, pl.ds(pl.multiple_of(i * C, C), C)] = total(iz)

    def b_d(i):
        b_send(sad, rad, da_s, da_r, sbd, rbd, db_s, db_r, outd, i)

    def b_n(i):
        b_send(san, ran, na_s, na_r, sbn, rbn, nb_s, nb_r, outn, i)

    def last(sb, rb, ss, rs, out, i):
        b_copy(sb, rb, ss, rs, i).wait_recv()
        out[:, pl.ds(pl.multiple_of(i * C, C), C)] += rb[i].astype(F32)

    def settle(i):
        @pl.when(i >= 1)
        def _():
            a_d(i - 1)

    def each(f):
        def g(i, _):
            f(i)
            return 0
        lax.fori_loop(0, nch, g, 0)

    def right_chunk(i):
        return remote(chunk(y_hbm, i), chunk(yr, i), yr_s.at[i], yr_r.at[i], n, l)

    @pl.when(even)
    def _():
        remote(bdv.at[1], bdvr, g_s.at[0], g_r.at[0], n, l).wait_recv()

        def first(i):
            right_chunk(i).wait_recv()
            make_z(i, True)

            @pl.when(plain_z)
            def _():
                z_up(i).start()

            @pl.when(src_z)
            def _():
                zw_direct(i).start()
                zw_out(i).start()

            for k in through:
                @pl.when(l == half + 2 * k)
                def _():
                    part_out(i, k).wait_recv()
                    part_on(i, k).start()
        each(first)

        def pass_z(i):
            @pl.when(rel_z)
            def _():
                zw_out(i).wait_recv()
                zw_on(i).start()

        def halves(i):
            make_x(y, i, ((lambda: bdo[0], xa), (lambda: bdo[1], xb)))
            for at, k in ((2, 0), (4, 1)):
                @pl.when(i == min(at, nch - 1))
                def _():
                    if k < nch:
                        pass_z(k)
        each(halves)

        def second(i):
            chi_cols(accd, i, xa, zt)
            scatter_d(i)
            for at, k in ((1, 2), (4, 3)):
                @pl.when(i == min(at, nch - 1))
                def _():
                    if k < nch:
                        pass_z(k)
        each(second)

        def third(i):
            @pl.when(has_dn)
            def _():
                @pl.when(lead)
                def _():
                    zw_direct(i).wait_recv()
                    zw_on(i).wait_recv()

                @pl.when(jnp.logical_not(lead))
                def _():
                    remote(zt.at[i], zin.at[i], z_s.at[i], z_r.at[i], n, l).wait_recv()
                chi_cols(accn, i, xb, zin)
                scatter_n_even(i)
            settle(i)

            if nch > 4:
                @pl.when(i == 1)
                def _():
                    pass_z(4)
        each(third)

    @pl.when(odd)
    def _():
        each(lambda i: make_x(y, i, ((lambda: bdo[0], xa),)))

        @pl.when(has_right)
        def _():
            remote(bdv.at[1], bdvr, g_s.at[0], g_r.at[0], n, l).wait_recv()

        @pl.when(has_up)
        def _():
            remote(bdo.at[1], bdor, g_s.at[1], g_r.at[1], n, l).wait_recv()

        def pass_y(i):
            @pl.when(rel_y)
            def _():
                yw_out(i).wait_recv()
                yw_on(i).start()
        pass_y(0)

        def step(i):
            @pl.when(has_right)
            def _():
                @pl.when(is_dst)
                def _():
                    for k in parts:
                        remote(cut(y_hbm, i, k), cut(yr, i, k), part_s.at[i, k], part_r.at[i, k], n, l).wait_recv()

                @pl.when(jnp.logical_not(is_dst))
                def _():
                    right_chunk(i).wait_recv()
                make_z(i, True)

            @pl.when(jnp.logical_not(has_right))
            def _():
                make_z(i, False)
            chi_cols(accd, i, xa, zt)
            scatter_d(i)

            @pl.when(i < nch - 1)
            def _():
                pass_y(i + 1)

            @pl.when(has_up)
            def _():
                @pl.when(tail)
                def _():
                    yw_direct(i).wait_recv()
                    yw_on(i).wait_recv()

                @pl.when(jnp.logical_not(tail))
                def _():
                    remote(chunk(y_hbm, i), chunk(yd, i), yd_s.at[i], yd_r.at[i], n, l).wait_recv()
                make_x(yd, i, ((lambda: bdor[...], xb),))

                def a(p, _):
                    chi_tile(accn, p, i, xb, zt)
                    return 0
                lax.fori_loop(0, i + 1, a, 0)

                def b(q, _):
                    chi_tile(accn, i, q, xb, zt)
                    return 0
                lax.fori_loop(0, i, b, 0)
            settle(i)
        each(step)

        @pl.when(has_up)
        def _():
            each(scatter_n_odd)

    a_d(nch - 1)

    @pl.when(has_up)
    def _():
        each(a_n)
    each(b_d)

    @pl.when(has_up)
    def _():
        each(b_n)
    each(lambda i: last(sbd, rbd, db_s, db_r, outd, i))

    @pl.when(has_up)
    def _():
        each(lambda i: last(sbn, rbn, nb_s, nb_r, outn, i))

    @pl.when(jnp.logical_not(has_up))
    def _():
        outn[...] = jnp.zeros_like(outn)

    @pl.when(has_left)
    def _():
        gv_left().wait_send()

    @pl.when(is_src)
    def _():
        for i in range(nch):
            part_direct(i).wait_send()
            for k in through:
                part_out(i, k).wait_send()

    for k in through:
        @pl.when(l == half + 2 * k)
        def _():
            for i in range(nch):
                part_on(i, k).wait_send()

    @pl.when(has_left & jnp.logical_not(is_src))
    def _():
        for i in range(nch):
            to_left(i).wait_send()

    @pl.when(has_dn & odd)
    def _():
        go_down().wait_send()

    @pl.when(plain_y)
    def _():
        for i in range(nch):
            to_down(i).wait_send()

    @pl.when(plain_z)
    def _():
        for i in range(nch):
            z_up(i).wait_send()

    @pl.when(src_y)
    def _():
        for i in range(nch):
            yw_direct(i).wait_send()
            yw_out(i).wait_send()

    @pl.when(src_z)
    def _():
        for i in range(nch):
            zw_direct(i).wait_send()
            zw_out(i).wait_send()

    @pl.when(rel_y)
    def _():
        for i in range(nch):
            yw_on(i).wait_send()

    @pl.when(rel_z)
    def _():
        for i in range(nch):
            zw_on(i).wait_send()

    def sent_d(i):
        d0(i).wait_send()
        b_copy(sbd, rbd, db_s, db_r, i).wait_send()
        for k in range(1, ny):
            a_copy(sad, rad, da_s, da_r, i, k).wait_send()
    each(sent_d)

    @pl.when(has_up)
    def _():
        def sent_n(i):
            b_copy(sbn, rbn, nb_s, nb_r, i).wait_send()
            for k in range(1, ny):
                a_copy(san, ran, na_s, na_r, i, k).wait_send()
        each(sent_n)

    @pl.when(has_dn & even)
    def _():
        each(lambda i: (n0_even(i, 0).wait_send(), n0_even(i, 1).wait_send()))

    @pl.when(has_up & odd)
    def _():
        each(lambda i: n0_odd(i).wait_send())


def solution(mesh):
    rows, cols = mesh.shape["row"], mesh.shape["col"]

    def body(three_centre, green_occ, green_vir, pair_live):
        aux, width = three_centre.shape[2:]
        tile = green_occ.shape[2]
        nch, own = aux // C, aux // cols
        half = cols // 2
        ny = half // 2
        nx = math.isqrt(rows)
        dma = pltpu.SemaphoreType.DMA
        vm = lambda *s: pltpu.VMEM(s, BF)
        out = pl.pallas_call(
            functools.partial(kernel, rows, cols, nx, tile),
            out_shape=jax.ShapeDtypeStruct((2, own, aux), F32),
            in_specs=[
                pl.BlockSpec(memory_space=pl.ANY),
                pl.BlockSpec(memory_space=pltpu.VMEM),
                pl.BlockSpec(memory_space=pltpu.VMEM),
                pl.BlockSpec(memory_space=pltpu.SMEM),
            ],
            out_specs=pl.BlockSpec(memory_space=pltpu.VMEM),
            scratch_shapes=[
                vm(2, W, W), vm(2, W, W),
                vm(aux, width), vm(aux, width), vm(aux, width),
                vm(nch, width, C), vm(nch, width, C),
                vm(aux, width), vm(aux, width),
                pltpu.VMEM((width, C), F32),
                pltpu.VMEM((nch, aux, C), F32), pltpu.VMEM((nch, aux, C), F32),
                vm(W, W), vm(W, W), vm(nch, C, max(size for _, size in shares(width, ny).values())), vm(nch, C, width // 2), vm(nch, width // 2, C),
                vm(nch, 2, half, own, C), vm(nch, 2, half, own, C), vm(nch, half, own, C), vm(nch, 2, half, own, C),
                vm(nch, ny, 2, own, C), vm(nch, ny, 2, own, C), vm(nch, ny, 2, own, C), vm(nch, ny, 2, own, C),
                vm(nch, own, C), vm(nch, own, C), vm(nch, own, C), vm(nch, own, C),
                *[dma((nch,))] * 7,
                dma((2,)), dma((2,)), dma((nch,)), dma((nch,)), dma((nch, ny)), dma((nch, ny)),
                dma((nch,)), dma((nch,)), dma((nch, 2)), dma((nch, 2)), dma((nch,)), dma((nch,)), dma((nch, 2)), dma((nch, 2)),
                dma((nch,)), dma((nch,)), dma((nch, 2)), dma((nch, 2)),
                *[dma((nch, ny))] * 4, *[dma((nch,))] * 4,
            ],
            compiler_params=pltpu.CompilerParams(
                collective_id=0, has_side_effects=True, vmem_limit_bytes=60 * 1024 * 1024),
        )(three_centre[0, 0], green_occ[0], green_vir[0], pair_live)
        return out[0][None], out[1][None]

    return jax.shard_map(
        body,
        mesh=mesh,
        in_specs=(
            P("row", "col", None, None),
            P("row", None, None, None),
            P("col", None, None, None),
            P("row", "col"),
        ),
        out_specs=(P("row", "col", None), P("row", "col", None)),
        check_vma=False,
    )
```

```python
import functools
import math

import jax
import jax.numpy as jnp
from jax import lax
from jax.experimental import pallas as pl
from jax.experimental.pallas import tpu as pltpu
from jax.sharding import PartitionSpec as P

MESH = pl.DeviceIdType.MESH
BF, F32 = jnp.bfloat16, jnp.float32
C = 128
W = 256
STEP = 1024


def dot_nt(a, b):
    return lax.dot_general(a, b, (((1,), (1,)), ((), ())), preferred_element_type=F32)


def dot_nn(a, b):
    return lax.dot_general(a, b, (((1,), (0,)), ((), ())), preferred_element_type=F32)


def shares(width, ny):
    weight = [2 if k == 1 and ny > 2 else 3 for k in range(ny)]
    edges = [width // 128 * sum(weight[:k]) // sum(weight) * 128 for k in range(ny + 1)]
    return {k: (edges[k], edges[k + 1] - edges[k]) for k in range(ny)}


def kernel(
    rows, cols, nx, tile,
    y_hbm, green_o, green_v, live, out2,
    bdo, bdv, y, yr, yd, zt, zin, xa, xb, t32, accd, accn, bdor, bdvr, rel, rely, relz,
    s0d, s0n, r0d, r0n, sad, san, rad, ran, sbd, sbn, rbd, rbn,
    loc_sem, yr_s, yr_r, yd_s, yd_r, z_s, z_r, g_s, g_r, rel_s, rel_r, part_s, part_r,
    ry_s, ry_r, yw_s, yw_r, rz_s, rz_r, zw_s, zw_r,
    d0_s, d0_r, n0_s, n0_r, da_s, da_r, na_s, na_r, db_s, db_r, nb_s, nb_r,
):
    n = lax.axis_index("row")
    l = lax.axis_index("col")
    aux, width = y_hbm.shape
    outd, outn = out2.at[0], out2.at[1]
    nch = aux // C
    own = aux // cols
    half = cols // 2
    ny = half // 2
    core = lax.rem(l, 2)
    iy = lax.rem(l // 2, ny)
    iz = l // half
    even = core == 0
    odd = core == 1
    has_up = n < rows - 1
    has_dn = n > 0
    has_right = l < cols - 1
    has_left = l > 0
    nblk = width // W
    parts = shares(width, ny)
    is_src = l == half
    is_dst = l == half - 1
    through = [k for k in parts if k > 0]
    is_rel = l < 0
    for k in through:
        is_rel = is_rel | (l == half + 2 * k)

    lead, tail = lax.rem(n, nx) == 0, lax.rem(n, nx) == nx - 1
    src_y, rel_y, dst_y = odd & lead & has_dn, odd & tail & (n >= nx), odd & tail & has_up
    src_z, rel_z, dst_z = even & tail & has_up, even & lead & (n + nx < rows), even & lead & has_dn

    barrier = pltpu.get_barrier_semaphore()

    def hello(cond, r, c):
        @pl.when(cond)
        def _():
            pl.semaphore_signal(barrier, inc=1, device_id=(r, c), device_id_type=MESH)
        return cond.astype(jnp.int32)

    def y_peer(k):
        return iz * half + lax.rem(iy + k, ny) * 2 + core

    z_peer = lax.rem(l + half, cols)
    always = l >= 0
    count = hello(has_left, n, l - 1) + hello(has_right, n, l + 1)
    count += hello(has_up, n + 1, l) + hello(has_dn, n - 1, l)
    count += hello(has_dn & even, n - 1, l + 1) + hello(has_up & odd, n + 1, l - 1)
    count += hello(always, n, z_peer) + hello(is_rel, n, half - 1)
    count += hello(src_y, n + nx - 1, l) + hello(rel_y, n - nx + 1, l)
    count += hello(rel_y, n - nx, l) + hello(dst_y, n + nx, l)
    count += hello(src_z, n - nx + 1, l) + hello(rel_z, n + nx - 1, l)
    count += hello(rel_z, n + nx, l) + hello(dst_z, n - nx, l)
    for k in range(1, ny):
        count += hello(always, n, y_peer(k))
    for k in through:
        count += hello(is_dst, n, half + 2 * k)
    on = live[0, 0].astype(F32)
    spot = [lax.shift_right_logical(lax.broadcasted_iota(jnp.int32, (W, W), k), tile.bit_length() - 1) for k in range(2)]
    for green, wide in ((green_o, bdo), (green_v, bdv)):
        for k in range(2):
            g = green[k].astype(F32) * on
            g = jnp.concatenate([g] * (W // tile), axis=1)
            g = jnp.concatenate([g] * (W // tile), axis=0)
            wide[k] = jnp.where(spot[0] == spot[1], g, 0.0).astype(BF)
    pl.semaphore_wait(barrier, count)

    def chunk(ref, i):
        return ref.at[pl.ds(i * C, C), :]

    def remote(src, dst, ss, rs, r, c):
        return pltpu.make_async_remote_copy(
            src_ref=src, dst_ref=dst, send_sem=ss, recv_sem=rs, device_id=(r, c), device_id_type=MESH)

    def to_left(i):
        return remote(chunk(y_hbm, i), chunk(yr, i), yr_s.at[i], yr_r.at[i], n, l - 1)

    def to_down(i):
        return remote(chunk(y_hbm, i), chunk(yd, i), yd_s.at[i], yd_r.at[i], n - 1, l)

    def z_up(i):
        return remote(zt.at[i], zin.at[i], z_s.at[i], z_r.at[i], n + 1, l)

    gv_left = lambda: remote(bdv.at[1], bdvr, g_s.at[0], g_r.at[0], n, l - 1)
    go_down = lambda: remote(bdo.at[1], bdor, g_s.at[1], g_r.at[1], n - 1, l)

    def cut(ref, i, k):
        at, size = parts[k]
        return ref.at[pl.ds(i * C, C), pl.ds(at, size)]

    def part_direct(i):
        return remote(cut(y_hbm, i, 0), cut(yr, i, 0), part_s.at[i, 0], part_r.at[i, 0], n, l - 1)

    def part_out(i, k):
        return remote(cut(y_hbm, i, k), rel.at[i, :, pl.ds(0, parts[k][1])], part_s.at[i, k], rel_r.at[i], n, half + 2 * k)

    def part_on(i, k):
        return remote(rel.at[i, :, pl.ds(0, parts[k][1])], cut(yr, i, k), rel_s.at[i], part_r.at[i, k], n, half - 1)

    @pl.when(has_left)
    def _():
        gv_left().start()

    @pl.when(is_src)
    def _():
        for i in range(nch):
            part_direct(i).start()
            for k in through:
                part_out(i, k).start()

    @pl.when(has_left & jnp.logical_not(is_src))
    def _():
        for i in range(nch):
            to_left(i).start()

    def side_y(ref, i, h):
        return ref.at[pl.ds(i * C, C), pl.ds(h * (width // 2), width // 2)]

    def side_z(ref, i, h):
        return ref.at[i, pl.ds(h * (width // 2), width // 2), :]

    def yw_direct(i):
        return remote(side_y(y_hbm, i, 0), side_y(yd, i, 0), yw_s.at[i, 0], yw_r.at[i, 0], n - 1, l)

    def yw_out(i):
        return remote(side_y(y_hbm, i, 1), rely.at[i], yw_s.at[i, 1], ry_r.at[i], n + nx - 1, l)

    def yw_on(i):
        return remote(rely.at[i], side_y(yd, i, 1), ry_s.at[i], yw_r.at[i, 1], n - nx, l)

    def zw_direct(i):
        return remote(side_z(zt, i, 0), side_z(zin, i, 0), zw_s.at[i, 0], zw_r.at[i, 0], n + 1, l)

    def zw_out(i):
        return remote(side_z(zt, i, 1), relz.at[i], zw_s.at[i, 1], rz_r.at[i], n - nx + 1, l)

    def zw_on(i):
        return remote(relz.at[i], side_z(zin, i, 1), rz_s.at[i], zw_r.at[i, 1], n + nx, l)

    plain_y = has_dn & odd & jnp.logical_not(lead)
    plain_z = has_up & even & jnp.logical_not(tail)

    @pl.when(has_dn & odd)
    def _():
        go_down().start()

    @pl.when(src_y)
    def _():
        for i in range(nch):
            if i == nch - 1:
                to_down(i).start()
            else:
                yw_direct(i).start()
                yw_out(i).start()

    @pl.when(plain_y)
    def _():
        for i in range(nch):
            to_down(i).start()

    def local(i):
        return pltpu.make_async_copy(chunk(y_hbm, i), chunk(y, i), loc_sem.at[i])

    for i in range(nch):
        local(i).start()
    for i in range(nch):
        local(i).wait()

    def spread(g):
        return jnp.concatenate(
            [t32[pl.ds(g * (W // tile) + j, tile, stride=tile), :] for j in range(W // tile)], axis=0)

    def make_z(i, right):
        def one(b, _):
            at = pl.ds(b * W, W)
            z = dot_nt(bdv[0], y[pl.ds(i * C, C), at])
            if right:
                z = z + dot_nt(bdvr[...], yr[pl.ds(i * C, C), at])
            t32[at, :] = z
            return 0
        lax.fori_loop(0, nblk, one, 0, unroll=True)

        def two(g, _):
            zt[i, pl.ds(g * W, W), :] = spread(g).astype(BF)
            return 0
        lax.fori_loop(0, nblk, two, 0, unroll=True)

    def make_x(src, i, targets):
        def one(b, _):
            at = pl.ds(b * W, W)
            t32[at, :] = jnp.transpose(src[pl.ds(i * C, C), at].astype(F32))
            return 0
        lax.fori_loop(0, nblk, one, 0, unroll=True)

        def two(g, _):
            part = jnp.transpose(spread(g)).astype(BF)
            for green, dst in targets:
                dst[pl.ds(i * C, C), pl.ds(g * W, W)] = dot_nn(part, green()).astype(BF)
            return 0
        lax.fori_loop(0, nblk, two, 0, unroll=True)

    def chi_cols(acc, i, x, z):
        acc[i] = jnp.zeros((aux, C), F32)

        def one(k, _):
            at = pl.ds(k * STEP, STEP)
            acc[i] += dot_nn(x[:, at], z[i, at, :])
            return 0
        lax.fori_loop(0, width // STEP, one, 0)

    def chi_tile(acc, p, q, x, z):
        at_p = pl.ds(p * C, C)
        acc[q, at_p, :] = dot_nn(x[at_p, :], z[q])

    def fill(acc, s0, i):
        for d in range(cols):
            s0[i, d % 2, d // 2] = acc[i, d * own:(d + 1) * own, :].astype(BF)

    def d0(i):
        return remote(s0d.at[i, 1 - core], r0d.at[i], d0_s.at[i], d0_r.at[i], n, l + 1 - 2 * core)

    def n0_even(i, c):
        return remote(s0n.at[i, c], r0n.at[i, 0], n0_s.at[i, c], n0_r.at[i, 0], n - 1, l + c)

    def n0_odd(i):
        return remote(s0n.at[i, 0], r0n.at[i, 1], n0_s.at[i, 0], n0_r.at[i, 1], n, l - 1)

    def scatter_d(i):
        fill(accd, s0d, i)
        d0(i).start()

    def scatter_n_even(i):
        fill(accn, s0n, i)
        n0_even(i, 0).start()
        n0_even(i, 1).start()

    def scatter_n_odd(i):
        fill(accn, s0n, i)
        n0_odd(i).start()

    def a_copy(sa, ra, ss, rs, i, k):
        to = lax.rem(iy + k, ny)
        return remote(sa.at[i, to], ra.at[i, iy], ss.at[i, to], rs.at[i, iy], n, y_peer(k))

    def a_send(first, second, sa, ra, ss, rs, i):
        for z in range(2):
            for k in range(ny):
                at = z * ny + k
                sa[i, k, z] = (first(at).astype(F32) + second(at).astype(F32)).astype(BF)
        ra[i, iy] = sa[i, iy]
        for k in range(1, ny):
            a_copy(sa, ra, ss, rs, i, k).start()

    def a_d(i):
        d0(i).wait_recv()
        a_send(lambda at: s0d[i, core, at], lambda at: r0d[i, at], sad, rad, da_s, da_r, i)

    def a_n(i):
        n0_even(i, 0).wait_recv()

        @pl.when(even)
        def _():
            n0_odd(i).wait_recv()
            a_send(lambda at: r0n[i, 0, at], lambda at: r0n[i, 1, at], san, ran, na_s, na_r, i)

        @pl.when(odd)
        def _():
            a_send(lambda at: r0n[i, 0, at], lambda at: s0n[i, 1, at], san, ran, na_s, na_r, i)

    def b_copy(sb, rb, ss, rs, i):
        return remote(sb.at[i], rb.at[i], ss.at[i], rs.at[i], n, z_peer)

    def b_send(sa, ra, sas, sar, sb, rb, ss, rs, out, i):
        for k in range(1, ny):
            j = lax.rem(iy + k, ny)
            remote(sa.at[i, j], ra.at[i, j], sas.at[i, j], sar.at[i, j], n, l).wait_recv()

        def total(z):
            t = ra[i, 0, z].astype(F32)
            for j in range(1, ny):
                t = t + ra[i, j, z].astype(F32)
            return t
        sb[i] = total(1 - iz).astype(BF)
        b_copy(sb, rb, ss, rs, i).start()
        out[:, pl.ds(pl.multiple_of(i * C, C), C)] = total(iz)

    def b_d(i):
        b_send(sad, rad, da_s, da_r, sbd, rbd, db_s, db_r, outd, i)

    def b_n(i):
        b_send(san, ran, na_s, na_r, sbn, rbn, nb_s, nb_r, outn, i)

    def last(sb, rb, ss, rs, out, i):
        b_copy(sb, rb, ss, rs, i).wait_recv()
        out[:, pl.ds(pl.multiple_of(i * C, C), C)] += rb[i].astype(F32)

    def settle(i):
        @pl.when(i >= 1)
        def _():
            a_d(i - 1)

        @pl.when(i == nch - 1)
        def _():
            lax.fori_loop(0, nch - 2, lambda k, c: (b_d(k), c)[1], 0)

    def each(f):
        def g(i, _):
            f(i)
            return 0
        lax.fori_loop(0, nch, g, 0)

    def right_chunk(i):
        return remote(chunk(y_hbm, i), chunk(yr, i), yr_s.at[i], yr_r.at[i], n, l)

    @pl.when(even)
    def _():
        remote(bdv.at[1], bdvr, g_s.at[0], g_r.at[0], n, l).wait_recv()

        def first(i):
            right_chunk(i).wait_recv()
            make_z(i, True)

            @pl.when(plain_z)
            def _():
                z_up(i).start()

            @pl.when(src_z)
            def _():
                zw_direct(i).start()
                zw_out(i).start()

            for k in through:
                @pl.when(l == half + 2 * k)
                def _():
                    part_out(i, k).wait_recv()
                    part_on(i, k).start()
        each(first)

        def pass_z(i):
            @pl.when(rel_z)
            def _():
                zw_out(i).wait_recv()
                zw_on(i).start()

        def halves(i):
            make_x(y, i, ((lambda: bdo[0], xa), (lambda: bdo[1], xb)))
            for at, k in ((2, 0), (4, 1)):
                @pl.when(i == min(at, nch - 1))
                def _():
                    if k < nch - 1:
                        pass_z(k)
        each(halves)

        def second(i):
            chi_cols(accd, i, xa, zt)
            scatter_d(i)
            for at, k in ((1, 2), (4, 3)):
                @pl.when(i == min(at, nch - 1))
                def _():
                    if k < nch - 1:
                        pass_z(k)
        each(second)

        def third(i):
            settle(i)

            @pl.when(has_dn)
            def _():
                @pl.when(lead)
                def _():
                    zw_direct(i).wait_recv()
                    zw_on(i).wait_recv()

                @pl.when(jnp.logical_not(lead))
                def _():
                    remote(zt.at[i], zin.at[i], z_s.at[i], z_r.at[i], n, l).wait_recv()
                chi_cols(accn, i, xb, zin)
                scatter_n_even(i)

            if nch > 4:
                @pl.when(i == 2)
                def _():
                    pass_z(4)

        each(third)

    @pl.when(odd)
    def _():
        each(lambda i: make_x(y, i, ((lambda: bdo[0], xa),)))

        @pl.when(has_right)
        def _():
            remote(bdv.at[1], bdvr, g_s.at[0], g_r.at[0], n, l).wait_recv()

        @pl.when(has_up)
        def _():
            remote(bdo.at[1], bdor, g_s.at[1], g_r.at[1], n, l).wait_recv()

        def pass_y(i):
            @pl.when(rel_y)
            def _():
                yw_out(i).wait_recv()
                yw_on(i).start()
        pass_y(0)

        def step(i):
            @pl.when(has_right)
            def _():
                @pl.when(is_dst)
                def _():
                    for k in parts:
                        remote(cut(y_hbm, i, k), cut(yr, i, k), part_s.at[i, k], part_r.at[i, k], n, l).wait_recv()

                @pl.when(jnp.logical_not(is_dst))
                def _():
                    right_chunk(i).wait_recv()
                make_z(i, True)

            @pl.when(jnp.logical_not(has_right))
            def _():
                make_z(i, False)
            chi_cols(accd, i, xa, zt)
            scatter_d(i)

            @pl.when(has_up)
            def _():
                def a(p, _):
                    chi_tile(accn, p, i, xb, zt)
                    return 0
                lax.fori_loop(0, i, a, 0)

            settle(i)

            @pl.when(i < nch - 2)
            def _():
                pass_y(i + 1)

            @pl.when(has_up)
            def _():
                @pl.when(tail & (i < nch - 1))
                def _():
                    yw_direct(i).wait_recv()
                    yw_on(i).wait_recv()

                @pl.when(jnp.logical_not(tail & (i < nch - 1)))
                def _():
                    remote(chunk(y_hbm, i), chunk(yd, i), yd_s.at[i], yd_r.at[i], n, l).wait_recv()
                make_x(yd, i, ((lambda: bdor[...], xb),))

                def b(q, _):
                    chi_tile(accn, i, q, xb, zt)

                    @pl.when(i == nch - 1)
                    def _():
                        scatter_n_odd(q)
                    return 0
                lax.fori_loop(0, i + 1, b, 0)
        each(step)

    a_d(nch - 1)

    @pl.when(has_up)
    def _():
        each(a_n)
    b_d(nch - 2)
    b_d(nch - 1)

    @pl.when(has_up)
    def _():
        each(b_n)
    each(lambda i: last(sbd, rbd, db_s, db_r, outd, i))

    @pl.when(has_up)
    def _():
        each(lambda i: last(sbn, rbn, nb_s, nb_r, outn, i))

    @pl.when(jnp.logical_not(has_up))
    def _():
        outn[...] = jnp.zeros_like(outn)

    @pl.when(has_left)
    def _():
        gv_left().wait_send()

    @pl.when(is_src)
    def _():
        for i in range(nch):
            part_direct(i).wait_send()
            for k in through:
                part_out(i, k).wait_send()

    for k in through:
        @pl.when(l == half + 2 * k)
        def _():
            for i in range(nch):
                part_on(i, k).wait_send()

    @pl.when(has_left & jnp.logical_not(is_src))
    def _():
        for i in range(nch):
            to_left(i).wait_send()

    @pl.when(has_dn & odd)
    def _():
        go_down().wait_send()

    @pl.when(plain_y)
    def _():
        for i in range(nch):
            to_down(i).wait_send()

    @pl.when(plain_z)
    def _():
        for i in range(nch):
            z_up(i).wait_send()

    @pl.when(src_y)
    def _():
        for i in range(nch - 1):
            yw_direct(i).wait_send()
            yw_out(i).wait_send()
        to_down(nch - 1).wait_send()

    @pl.when(src_z)
    def _():
        for i in range(nch):
            zw_direct(i).wait_send()
            zw_out(i).wait_send()

    @pl.when(rel_y)
    def _():
        for i in range(nch - 1):
            yw_on(i).wait_send()

    @pl.when(rel_z)
    def _():
        for i in range(nch):
            zw_on(i).wait_send()

    def sent_d(i):
        d0(i).wait_send()
        b_copy(sbd, rbd, db_s, db_r, i).wait_send()
        for k in range(1, ny):
            a_copy(sad, rad, da_s, da_r, i, k).wait_send()
    each(sent_d)

    @pl.when(has_up)
    def _():
        def sent_n(i):
            b_copy(sbn, rbn, nb_s, nb_r, i).wait_send()
            for k in range(1, ny):
                a_copy(san, ran, na_s, na_r, i, k).wait_send()
        each(sent_n)

    @pl.when(has_dn & even)
    def _():
        each(lambda i: (n0_even(i, 0).wait_send(), n0_even(i, 1).wait_send()))

    @pl.when(has_up & odd)
    def _():
        each(lambda i: n0_odd(i).wait_send())


def solution(mesh):
    rows, cols = mesh.shape["row"], mesh.shape["col"]

    def body(three_centre, green_occ, green_vir, pair_live):
        aux, width = three_centre.shape[2:]
        tile = green_occ.shape[2]
        nch, own = aux // C, aux // cols
        half = cols // 2
        ny = half // 2
        nx = math.isqrt(rows)
        dma = pltpu.SemaphoreType.DMA
        vm = lambda *s: pltpu.VMEM(s, BF)
        out = pl.pallas_call(
            functools.partial(kernel, rows, cols, nx, tile),
            out_shape=jax.ShapeDtypeStruct((2, own, aux), F32),
            in_specs=[
                pl.BlockSpec(memory_space=pl.ANY),
                pl.BlockSpec(memory_space=pltpu.VMEM),
                pl.BlockSpec(memory_space=pltpu.VMEM),
                pl.BlockSpec(memory_space=pltpu.SMEM),
            ],
            out_specs=pl.BlockSpec(memory_space=pltpu.VMEM),
            scratch_shapes=[
                vm(2, W, W), vm(2, W, W),
                vm(aux, width), vm(aux, width), vm(aux, width),
                vm(nch, width, C), vm(nch, width, C),
                vm(aux, width), vm(aux, width),
                pltpu.VMEM((width, C), F32),
                pltpu.VMEM((nch, aux, C), F32), pltpu.VMEM((nch, aux, C), F32),
                vm(W, W), vm(W, W), vm(nch, C, max(size for _, size in shares(width, ny).values())), vm(nch, C, width // 2), vm(nch, width // 2, C),
                vm(nch, 2, half, own, C), vm(nch, 2, half, own, C), vm(nch, half, own, C), vm(nch, 2, half, own, C),
                vm(nch, ny, 2, own, C), vm(nch, ny, 2, own, C), vm(nch, ny, 2, own, C), vm(nch, ny, 2, own, C),
                vm(nch, own, C), vm(nch, own, C), vm(nch, own, C), vm(nch, own, C),
                *[dma((nch,))] * 7,
                dma((2,)), dma((2,)), dma((nch,)), dma((nch,)), dma((nch, ny)), dma((nch, ny)),
                dma((nch,)), dma((nch,)), dma((nch, 2)), dma((nch, 2)), dma((nch,)), dma((nch,)), dma((nch, 2)), dma((nch, 2)),
                dma((nch,)), dma((nch,)), dma((nch, 2)), dma((nch, 2)),
                *[dma((nch, ny))] * 4, *[dma((nch,))] * 4,
            ],
            compiler_params=pltpu.CompilerParams(
                collective_id=0, has_side_effects=True, vmem_limit_bytes=60 * 1024 * 1024),
        )(three_centre[0, 0], green_occ[0], green_vir[0], pair_live)
        return out[0][None], out[1][None]

    return jax.shard_map(
        body,
        mesh=mesh,
        in_specs=(
            P("row", "col", None, None),
            P("row", None, None, None),
            P("col", None, None, None),
            P("row", "col"),
        ),
        out_specs=(P("row", "col", None), P("row", "col", None)),
        check_vma=False,
    )
```

```python
import functools
import math

import jax
import jax.numpy as jnp
from jax import lax
from jax.experimental import pallas as pl
from jax.experimental.pallas import tpu as pltpu
from jax.sharding import PartitionSpec as P

MESH = pl.DeviceIdType.MESH
BF, F32 = jnp.bfloat16, jnp.float32
C = 128
W = 256
STEP = 1024


def dot_nt(a, b):
    return lax.dot_general(a, b, (((1,), (1,)), ((), ())), preferred_element_type=F32)


def dot_nn(a, b):
    return lax.dot_general(a, b, (((1,), (0,)), ((), ())), preferred_element_type=F32)


def shares(width, ny):
    weight = [1] * ny
    edges = [width // 128 * sum(weight[:k]) // sum(weight) * 128 for k in range(ny + 1)]
    return {k: (edges[k], edges[k + 1] - edges[k]) for k in range(ny)}


def kernel(
    rows, cols, nx, tile,
    y_hbm, green_o, green_v, live, out2,
    bdo, bdv, y, yr, yd, zt, zin, xa, xb, t32, accd, accn, bdor, bdvr, rel, rely, relz,
    s0d, s0n, r0d, r0n, sad, san, rad, ran, sbd, sbn, rbd, rbn,
    loc_sem, yr_s, yr_r, yd_s, yd_r, z_s, z_r, g_s, g_r, rel_s, rel_r, part_s, part_r,
    ry_s, ry_r, yw_s, yw_r, rz_s, rz_r, zw_s, zw_r,
    d0_s, d0_r, n0_s, n0_r, da_s, da_r, na_s, na_r, db_s, db_r, nb_s, nb_r,
):
    n = lax.axis_index("row")
    l = lax.axis_index("col")
    aux, width = y_hbm.shape
    outd, outn = out2.at[0], out2.at[1]
    nch = aux // C
    own = aux // cols
    half = cols // 2
    ny = half // 2
    core = lax.rem(l, 2)
    iy = lax.rem(l // 2, ny)
    iz = l // half
    even = core == 0
    odd = core == 1
    has_up = n < rows - 1
    has_dn = n > 0
    has_right = l < cols - 1
    has_left = l > 0
    nblk = width // W
    parts = shares(width, ny)
    is_src = l == half
    is_dst = l == half - 1
    through = [k for k in parts if k > 0]
    is_rel = l < 0
    for k in through:
        is_rel = is_rel | (l == half + 2 * k)

    lead, tail = lax.rem(n, nx) == 0, lax.rem(n, nx) == nx - 1
    src_y, rel_y, dst_y = odd & lead & has_dn, even & tail & (n >= nx), odd & tail & has_up
    src_z, rel_z, dst_z = even & tail & has_up, even & lead & (n + nx < rows), even & lead & has_dn

    barrier = pltpu.get_barrier_semaphore()

    def hello(cond, r, c):
        @pl.when(cond)
        def _():
            pl.semaphore_signal(barrier, inc=1, device_id=(r, c), device_id_type=MESH)
        return cond.astype(jnp.int32)

    def y_peer(k):
        return iz * half + lax.rem(iy + k, ny) * 2 + core

    z_peer = lax.rem(l + half, cols)
    always = l >= 0
    count = hello(has_left, n, l - 1) + hello(has_right, n, l + 1)
    count += hello(has_up, n + 1, l) + hello(has_dn, n - 1, l)
    count += hello(has_dn & even, n - 1, l + 1) + hello(has_up & odd, n + 1, l - 1)
    count += hello(always, n, z_peer) + hello(is_rel, n, half - 1)
    count += hello(src_y, n + nx - 1, l - 1) + hello(rel_y, n - nx + 1, l + 1)
    count += hello(rel_y, n - nx, l + 1) + hello(dst_y, n + nx, l - 1)
    count += hello(src_z, n - nx + 1, l) + hello(rel_z, n + nx - 1, l)
    count += hello(rel_z, n + nx, l) + hello(dst_z, n - nx, l)
    for k in range(1, ny):
        count += hello(always, n, y_peer(k))
    for k in through:
        count += hello(is_dst, n, half + 2 * k)
    on = live[0, 0].astype(F32)
    spot = [lax.shift_right_logical(lax.broadcasted_iota(jnp.int32, (W, W), k), tile.bit_length() - 1) for k in range(2)]
    for green, wide in ((green_o, bdo), (green_v, bdv)):
        for k in range(2):
            g = green[k].astype(F32) * on
            g = jnp.concatenate([g] * (W // tile), axis=1)
            g = jnp.concatenate([g] * (W // tile), axis=0)
            wide[k] = jnp.where(spot[0] == spot[1], g, 0.0).astype(BF)
    pl.semaphore_wait(barrier, count)

    def chunk(ref, i):
        return ref.at[pl.ds(i * C, C), :]

    def remote(src, dst, ss, rs, r, c):
        return pltpu.make_async_remote_copy(
            src_ref=src, dst_ref=dst, send_sem=ss, recv_sem=rs, device_id=(r, c), device_id_type=MESH)

    def to_left(i):
        return remote(chunk(y_hbm, i), chunk(yr, i), yr_s.at[i], yr_r.at[i], n, l - 1)

    def to_down(i):
        return remote(chunk(y_hbm, i), chunk(yd, i), yd_s.at[i], yd_r.at[i], n - 1, l)

    def z_up(i):
        return remote(zt.at[i], zin.at[i], z_s.at[i], z_r.at[i], n + 1, l)

    gv_left = lambda: remote(bdv.at[1], bdvr, g_s.at[0], g_r.at[0], n, l - 1)
    go_down = lambda: remote(bdo.at[1], bdor, g_s.at[1], g_r.at[1], n - 1, l)

    def cut(ref, i, k):
        at, size = parts[k]
        return ref.at[pl.ds(i * C, C), pl.ds(at, size)]

    def part_direct(i):
        return remote(cut(y_hbm, i, 0), cut(yr, i, 0), part_s.at[i, 0], part_r.at[i, 0], n, l - 1)

    def part_out(i, k):
        return remote(cut(y_hbm, i, k), rel.at[i, :, pl.ds(0, parts[k][1])], part_s.at[i, k], rel_r.at[i], n, half + 2 * k)

    def part_on(i, k):
        return remote(rel.at[i, :, pl.ds(0, parts[k][1])], cut(yr, i, k), rel_s.at[i], part_r.at[i, k], n, half - 1)

    @pl.when(has_left)
    def _():
        gv_left().start()

    @pl.when(is_src)
    def _():
        for i in range(nch):
            part_direct(i).start()
            for k in through:
                part_out(i, k).start()

    @pl.when(has_left & jnp.logical_not(is_src))
    def _():
        for i in range(nch):
            to_left(i).start()

    def side_y(ref, i, h):
        return ref.at[pl.ds(i * C, C), pl.ds(h * (width // 2), width // 2)]

    def side_z(ref, i, h):
        return ref.at[i, pl.ds(h * (width // 2), width // 2), :]

    def yw_direct(i):
        return remote(side_y(y_hbm, i, 0), side_y(yd, i, 0), yw_s.at[i, 0], yw_r.at[i, 0], n - 1, l)

    def yw_out(i):
        return remote(side_y(y_hbm, i, 1), rely.at[i], yw_s.at[i, 1], ry_r.at[i], n + nx - 1, l - 1)

    def yw_on(i):
        return remote(rely.at[i], side_y(yd, i, 1), ry_s.at[i], yw_r.at[i, 1], n - nx, l + 1)

    def zw_direct(i):
        return remote(side_z(zt, i, 0), side_z(zin, i, 0), zw_s.at[i, 0], zw_r.at[i, 0], n + 1, l)

    def zw_out(i):
        return remote(side_z(zt, i, 1), relz.at[i], zw_s.at[i, 1], rz_r.at[i], n - nx + 1, l)

    def zw_on(i):
        return remote(relz.at[i], side_z(zin, i, 1), rz_s.at[i], zw_r.at[i, 1], n + nx, l)

    plain_y = has_dn & odd & jnp.logical_not(lead)
    plain_z = has_up & even & jnp.logical_not(tail)

    @pl.when(has_dn & odd)
    def _():
        go_down().start()

    @pl.when(src_y)
    def _():
        for i in range(nch):
            yw_direct(i).start()
            yw_out(i).start()

    @pl.when(plain_y)
    def _():
        for i in range(nch):
            to_down(i).start()

    def local(i):
        return pltpu.make_async_copy(chunk(y_hbm, i), chunk(y, i), loc_sem.at[i])

    for i in range(nch):
        local(i).start()
    for i in range(nch):
        local(i).wait()

    def spread(g):
        return jnp.concatenate(
            [t32[pl.ds(g * (W // tile) + j, tile, stride=tile), :] for j in range(W // tile)], axis=0)

    def make_z(i, right):
        def one(b, _):
            at = pl.ds(b * W, W)
            z = dot_nt(bdv[0], y[pl.ds(i * C, C), at])
            if right:
                z = z + dot_nt(bdvr[...], yr[pl.ds(i * C, C), at])
            t32[at, :] = z
            return 0
        lax.fori_loop(0, nblk, one, 0, unroll=True)

        def two(g, _):
            zt[i, pl.ds(g * W, W), :] = spread(g).astype(BF)
            return 0
        lax.fori_loop(0, nblk, two, 0, unroll=True)

    def make_x(src, i, targets):
        def one(b, _):
            at = pl.ds(b * W, W)
            t32[at, :] = jnp.transpose(src[pl.ds(i * C, C), at].astype(F32))
            return 0
        lax.fori_loop(0, nblk, one, 0, unroll=True)

        def two(g, _):
            part = jnp.transpose(spread(g)).astype(BF)
            for green, dst in targets:
                dst[pl.ds(i * C, C), pl.ds(g * W, W)] = dot_nn(part, green()).astype(BF)
            return 0
        lax.fori_loop(0, nblk, two, 0, unroll=True)

    def chi_cols(acc, i, x, z):
        acc[i] = jnp.zeros((aux, C), F32)

        def one(k, _):
            at = pl.ds(k * STEP, STEP)
            acc[i] += dot_nn(x[:, at], z[i, at, :])
            return 0
        lax.fori_loop(0, width // STEP, one, 0)

    def chi_tile(acc, p, q, x, z):
        at_p = pl.ds(p * C, C)
        acc[q, at_p, :] = dot_nn(x[at_p, :], z[q])

    def fill(acc, s0, i):
        for d in range(cols):
            s0[i, d % 2, d // 2] = acc[i, d * own:(d + 1) * own, :].astype(BF)

    def d0(i):
        return remote(s0d.at[i, 1 - core], r0d.at[i], d0_s.at[i], d0_r.at[i], n, l + 1 - 2 * core)

    def n0_even(i, c):
        return remote(s0n.at[i, c], r0n.at[i, 0], n0_s.at[i, c], n0_r.at[i, 0], n - 1, l + c)

    def n0_odd(i):
        return remote(s0n.at[i, 0], r0n.at[i, 1], n0_s.at[i, 0], n0_r.at[i, 1], n, l - 1)

    def scatter_d(i):
        fill(accd, s0d, i)
        d0(i).start()

    def scatter_n_even(i):
        fill(accn, s0n, i)
        n0_even(i, 0).start()
        n0_even(i, 1).start()

    def scatter_n_odd(i):
        fill(accn, s0n, i)
        n0_odd(i).start()

    def a_copy(sa, ra, ss, rs, i, k):
        to = lax.rem(iy + k, ny)
        return remote(sa.at[i, to], ra.at[i, iy], ss.at[i, to], rs.at[i, iy], n, y_peer(k))

    def a_send(first, second, sa, ra, ss, rs, i):
        for z in range(2):
            for k in range(ny):
                at = z * ny + k
                sa[i, k, z] = (first(at).astype(F32) + second(at).astype(F32)).astype(BF)
        ra[i, iy] = sa[i, iy]
        for k in range(1, ny):
            a_copy(sa, ra, ss, rs, i, k).start()

    def a_d(i):
        d0(i).wait_recv()
        a_send(lambda at: s0d[i, core, at], lambda at: r0d[i, at], sad, rad, da_s, da_r, i)

    def a_n(i):
        n0_even(i, 0).wait_recv()

        @pl.when(even)
        def _():
            n0_odd(i).wait_recv()
            a_send(lambda at: r0n[i, 0, at], lambda at: r0n[i, 1, at], san, ran, na_s, na_r, i)

        @pl.when(odd)
        def _():
            a_send(lambda at: r0n[i, 0, at], lambda at: s0n[i, 1, at], san, ran, na_s, na_r, i)

    def b_copy(sb, rb, ss, rs, i):
        return remote(sb.at[i], rb.at[i], ss.at[i], rs.at[i], n, z_peer)

    def b_send(sa, ra, sas, sar, sb, rb, ss, rs, out, i):
        for k in range(1, ny):
            j = lax.rem(iy + k, ny)
            remote(sa.at[i, j], ra.at[i, j], sas.at[i, j], sar.at[i, j], n, l).wait_recv()

        def total(z):
            t = ra[i, 0, z].astype(F32)
            for j in range(1, ny):
                t = t + ra[i, j, z].astype(F32)
            return t
        sb[i] = total(1 - iz).astype(BF)
        b_copy(sb, rb, ss, rs, i).start()
        out[:, pl.ds(pl.multiple_of(i * C, C), C)] = total(iz)

    def b_d(i):
        b_send(sad, rad, da_s, da_r, sbd, rbd, db_s, db_r, outd, i)

    def b_n(i):
        b_send(san, ran, na_s, na_r, sbn, rbn, nb_s, nb_r, outn, i)

    def last(sb, rb, ss, rs, out, i):
        b_copy(sb, rb, ss, rs, i).wait_recv()
        out[:, pl.ds(pl.multiple_of(i * C, C), C)] += rb[i].astype(F32)

    def settle(i):
        @pl.when(i >= 1)
        def _():
            a_d(i - 1)

        @pl.when(i == nch - 1)
        def _():
            lax.fori_loop(0, nch - 2, lambda k, c: (b_d(k), c)[1], 0)

    def each(f):
        def g(i, _):
            f(i)
            return 0
        lax.fori_loop(0, nch, g, 0)

    def right_chunk(i):
        return remote(chunk(y_hbm, i), chunk(yr, i), yr_s.at[i], yr_r.at[i], n, l)

    @pl.when(even)
    def _():
        remote(bdv.at[1], bdvr, g_s.at[0], g_r.at[0], n, l).wait_recv()

        def first(i):
            right_chunk(i).wait_recv()
            make_z(i, True)

            @pl.when(plain_z)
            def _():
                z_up(i).start()

            @pl.when(src_z)
            def _():
                zw_direct(i).start()
                zw_out(i).start()

            for k in through:
                @pl.when(l == half + 2 * k)
                def _():
                    part_out(i, k).wait_recv()
                    part_on(i, k).start()
        each(first)

        def pass_on(i):
            @pl.when(rel_y)
            def _():
                yw_out(i).wait_recv()
                yw_on(i).start()

            @pl.when(rel_z)
            def _():
                zw_out(i).wait_recv()
                zw_on(i).start()

        def halves(i):
            make_x(y, i, ((lambda: bdo[0], xa), (lambda: bdo[1], xb)))
            for at, k in ((2, 0), (4, 1)):
                @pl.when(i == min(at, nch - 1))
                def _():
                    if k < nch:
                        pass_on(k)
        each(halves)

        def second(i):
            chi_cols(accd, i, xa, zt)
            scatter_d(i)
            for at, k in ((1, 2), (4, 3)):
                @pl.when(i == min(at, nch - 1))
                def _():
                    if k < nch:
                        pass_on(k)
        each(second)

        def third(i):
            settle(i)

            @pl.when(has_dn)
            def _():
                @pl.when(lead)
                def _():
                    zw_direct(i).wait_recv()
                    zw_on(i).wait_recv()

                @pl.when(jnp.logical_not(lead))
                def _():
                    remote(zt.at[i], zin.at[i], z_s.at[i], z_r.at[i], n, l).wait_recv()
                chi_cols(accn, i, xb, zin)
                scatter_n_even(i)

            if nch > 4:
                @pl.when(i == 3)
                def _():
                    pass_on(4)
        each(third)

    @pl.when(odd)
    def _():
        each(lambda i: make_x(y, i, ((lambda: bdo[0], xa),)))

        @pl.when(has_right)
        def _():
            remote(bdv.at[1], bdvr, g_s.at[0], g_r.at[0], n, l).wait_recv()

        @pl.when(has_up)
        def _():
            remote(bdo.at[1], bdor, g_s.at[1], g_r.at[1], n, l).wait_recv()

        def step(i):
            @pl.when(has_right)
            def _():
                @pl.when(is_dst)
                def _():
                    for k in parts:
                        remote(cut(y_hbm, i, k), cut(yr, i, k), part_s.at[i, k], part_r.at[i, k], n, l).wait_recv()

                @pl.when(jnp.logical_not(is_dst))
                def _():
                    right_chunk(i).wait_recv()
                make_z(i, True)

            @pl.when(jnp.logical_not(has_right))
            def _():
                make_z(i, False)
            chi_cols(accd, i, xa, zt)
            scatter_d(i)

            @pl.when(has_up)
            def _():
                def a(p, _):
                    chi_tile(accn, p, i, xb, zt)
                    return 0
                lax.fori_loop(0, i, a, 0)

            settle(i)

            @pl.when(has_up)
            def _():
                @pl.when(tail)
                def _():
                    yw_direct(i).wait_recv()
                    yw_on(i).wait_recv()

                @pl.when(jnp.logical_not(tail))
                def _():
                    remote(chunk(y_hbm, i), chunk(yd, i), yd_s.at[i], yd_r.at[i], n, l).wait_recv()
                make_x(yd, i, ((lambda: bdor[...], xb),))

                def b(q, _):
                    chi_tile(accn, i, q, xb, zt)

                    @pl.when(i == nch - 1)
                    def _():
                        scatter_n_odd(q)
                    return 0
                lax.fori_loop(0, i + 1, b, 0)
        each(step)

    a_d(nch - 1)

    @pl.when(has_up)
    def _():
        each(a_n)
    b_d(nch - 2)
    b_d(nch - 1)

    @pl.when(has_up)
    def _():
        each(b_n)
    each(lambda i: last(sbd, rbd, db_s, db_r, outd, i))

    @pl.when(has_up)
    def _():
        each(lambda i: last(sbn, rbn, nb_s, nb_r, outn, i))

    @pl.when(jnp.logical_not(has_up))
    def _():
        outn[...] = jnp.zeros_like(outn)

    @pl.when(has_left)
    def _():
        gv_left().wait_send()

    @pl.when(is_src)
    def _():
        for i in range(nch):
            part_direct(i).wait_send()
            for k in through:
                part_out(i, k).wait_send()

    for k in through:
        @pl.when(l == half + 2 * k)
        def _():
            for i in range(nch):
                part_on(i, k).wait_send()

    @pl.when(has_left & jnp.logical_not(is_src))
    def _():
        for i in range(nch):
            to_left(i).wait_send()

    @pl.when(has_dn & odd)
    def _():
        go_down().wait_send()

    @pl.when(plain_y)
    def _():
        for i in range(nch):
            to_down(i).wait_send()

    @pl.when(plain_z)
    def _():
        for i in range(nch):
            z_up(i).wait_send()

    @pl.when(src_y)
    def _():
        for i in range(nch):
            yw_direct(i).wait_send()
            yw_out(i).wait_send()

    @pl.when(src_z)
    def _():
        for i in range(nch):
            zw_direct(i).wait_send()
            zw_out(i).wait_send()

    @pl.when(rel_y)
    def _():
        for i in range(nch):
            yw_on(i).wait_send()

    @pl.when(rel_z)
    def _():
        for i in range(nch):
            zw_on(i).wait_send()

    def sent_d(i):
        d0(i).wait_send()
        b_copy(sbd, rbd, db_s, db_r, i).wait_send()
        for k in range(1, ny):
            a_copy(sad, rad, da_s, da_r, i, k).wait_send()
    each(sent_d)

    @pl.when(has_up)
    def _():
        def sent_n(i):
            b_copy(sbn, rbn, nb_s, nb_r, i).wait_send()
            for k in range(1, ny):
                a_copy(san, ran, na_s, na_r, i, k).wait_send()
        each(sent_n)

    @pl.when(has_dn & even)
    def _():
        each(lambda i: (n0_even(i, 0).wait_send(), n0_even(i, 1).wait_send()))

    @pl.when(has_up & odd)
    def _():
        each(lambda i: n0_odd(i).wait_send())


def solution(mesh):
    rows, cols = mesh.shape["row"], mesh.shape["col"]

    def body(three_centre, green_occ, green_vir, pair_live):
        aux, width = three_centre.shape[2:]
        tile = green_occ.shape[2]
        nch, own = aux // C, aux // cols
        half = cols // 2
        ny = half // 2
        nx = math.isqrt(rows)
        dma = pltpu.SemaphoreType.DMA
        vm = lambda *s: pltpu.VMEM(s, BF)
        out = pl.pallas_call(
            functools.partial(kernel, rows, cols, nx, tile),
            out_shape=jax.ShapeDtypeStruct((2, own, aux), F32),
            in_specs=[
                pl.BlockSpec(memory_space=pl.ANY),
                pl.BlockSpec(memory_space=pltpu.VMEM),
                pl.BlockSpec(memory_space=pltpu.VMEM),
                pl.BlockSpec(memory_space=pltpu.SMEM),
            ],
            out_specs=pl.BlockSpec(memory_space=pltpu.VMEM),
            scratch_shapes=[
                vm(2, W, W), vm(2, W, W),
                vm(aux, width), vm(aux, width), vm(aux, width),
                vm(nch, width, C), vm(nch, width, C),
                vm(aux, width), vm(aux, width),
                pltpu.VMEM((width, C), F32),
                pltpu.VMEM((nch, aux, C), F32), pltpu.VMEM((nch, aux, C), F32),
                vm(W, W), vm(W, W), vm(nch, C, max(size for _, size in shares(width, ny).values())), vm(nch, C, width // 2), vm(nch, width // 2, C),
                vm(nch, 2, half, own, C), vm(nch, 2, half, own, C), vm(nch, half, own, C), vm(nch, 2, half, own, C),
                vm(nch, ny, 2, own, C), vm(nch, ny, 2, own, C), vm(nch, ny, 2, own, C), vm(nch, ny, 2, own, C),
                vm(nch, own, C), vm(nch, own, C), vm(nch, own, C), vm(nch, own, C),
                *[dma((nch,))] * 7,
                dma((2,)), dma((2,)), dma((nch,)), dma((nch,)), dma((nch, ny)), dma((nch, ny)),
                dma((nch,)), dma((nch,)), dma((nch, 2)), dma((nch, 2)), dma((nch,)), dma((nch,)), dma((nch, 2)), dma((nch, 2)),
                dma((nch,)), dma((nch,)), dma((nch, 2)), dma((nch, 2)),
                *[dma((nch, ny))] * 4, *[dma((nch,))] * 4,
            ],
            compiler_params=pltpu.CompilerParams(
                collective_id=0, has_side_effects=True, vmem_limit_bytes=60 * 1024 * 1024),
        )(three_centre[0, 0], green_occ[0], green_vir[0], pair_live)
        return out[0][None], out[1][None]

    return jax.shard_map(
        body,
        mesh=mesh,
        in_specs=(
            P("row", "col", None, None),
            P("row", None, None, None),
            P("col", None, None, None),
            P("row", "col"),
        ),
        out_specs=(P("row", "col", None), P("row", "col", None)),
        check_vma=False,
    )
```

```python
import functools
import math

import jax
import jax.numpy as jnp
from jax import lax
from jax.experimental import pallas as pl
from jax.experimental.pallas import tpu as pltpu
from jax.sharding import PartitionSpec as P

MESH = pl.DeviceIdType.MESH
BF, F32 = jnp.bfloat16, jnp.float32
C = 128
W = 256
STEP = 1024


def dot_nt(a, b):
    return lax.dot_general(a, b, (((1,), (1,)), ((), ())), preferred_element_type=F32)


def dot_nn(a, b):
    return lax.dot_general(a, b, (((1,), (0,)), ((), ())), preferred_element_type=F32)


def shares(width, ny):
    weight = [1] * ny
    edges = [width // 128 * sum(weight[:k]) // sum(weight) * 128 for k in range(ny + 1)]
    return {k: (edges[k], edges[k + 1] - edges[k]) for k in range(ny)}


def kernel(
    rows, cols, nx, tile,
    y_hbm, green_o, green_v, live, out2,
    bdo, bdv, y, yr, yd, zt, zin, xa, xb, t32, accd, accn, bdor, bdvr, rel, rely, relz,
    s0d, s0n, r0d, r0n, sad, san, rad, ran, sbd, sbn, rbd, rbn,
    loc_sem, yr_s, yr_r, yd_s, yd_r, z_s, z_r, g_s, g_r, rel_s, rel_r, part_s, part_r,
    ry_s, ry_r, yw_s, yw_r, rz_s, rz_r, zw_s, zw_r,
    d0_s, d0_r, n0_s, n0_r, da_s, da_r, na_s, na_r, db_s, db_r, nb_s, nb_r,
):
    n = lax.axis_index("row")
    l = lax.axis_index("col")
    aux, width = y_hbm.shape
    outd, outn = out2.at[0], out2.at[1]
    nch = aux // C
    own = aux // cols
    half = cols // 2
    ny = half // 2
    core = lax.rem(l, 2)
    iy = lax.rem(l // 2, ny)
    iz = l // half
    even = core == 0
    odd = core == 1
    has_up = n < rows - 1
    has_dn = n > 0
    has_right = l < cols - 1
    has_left = l > 0
    nblk = width // W
    parts = shares(width, ny)
    is_src = l == half
    is_dst = l == half - 1
    through = [k for k in parts if k > 0]
    is_rel = l < 0
    for k in through:
        is_rel = is_rel | (l == half + 2 * k)

    lead, tail = lax.rem(n, nx) == 0, lax.rem(n, nx) == nx - 1
    src_y, rel_y, dst_y = odd & lead & has_dn, even & tail & (n >= nx), odd & tail & has_up
    src_z, rel_z, dst_z = even & tail & has_up, even & lead & (n + nx < rows), even & lead & has_dn

    def chunk(ref, i):
        return ref.at[pl.ds(i * C, C), :]

    def local(i):
        return pltpu.make_async_copy(chunk(y_hbm, i), chunk(y, i), loc_sem.at[i])

    for i in range(nch):
        local(i).start()

    barrier = pltpu.get_barrier_semaphore()

    def hello(cond, r, c):
        @pl.when(cond)
        def _():
            pl.semaphore_signal(barrier, inc=1, device_id=(r, c), device_id_type=MESH)
        return cond.astype(jnp.int32)

    def y_peer(k):
        return iz * half + lax.rem(iy + k, ny) * 2 + core

    z_peer = lax.rem(l + half, cols)
    always = l >= 0
    count = hello(has_left, n, l - 1) + hello(has_right, n, l + 1)
    count += hello(has_up, n + 1, l) + hello(has_dn, n - 1, l)
    count += hello(has_dn & even, n - 1, l + 1) + hello(has_up & odd, n + 1, l - 1)
    count += hello(always, n, z_peer) + hello(is_rel, n, half - 1)
    count += hello(src_y, n + nx - 1, l - 1) + hello(rel_y, n - nx + 1, l + 1)
    count += hello(rel_y, n - nx, l + 1) + hello(dst_y, n + nx, l - 1)
    count += hello(src_z, n - nx + 1, l) + hello(rel_z, n + nx - 1, l)
    count += hello(rel_z, n + nx, l) + hello(dst_z, n - nx, l)
    for k in range(1, ny):
        count += hello(always, n, y_peer(k))
    for k in through:
        count += hello(is_dst, n, half + 2 * k)
    on = live[0, 0].astype(F32)
    spot = [lax.shift_right_logical(lax.broadcasted_iota(jnp.int32, (W, W), k), tile.bit_length() - 1) for k in range(2)]
    for green, wide in ((green_o, bdo), (green_v, bdv)):
        for k in range(2):
            g = green[k].astype(F32) * on
            g = jnp.concatenate([g] * (W // tile), axis=1)
            g = jnp.concatenate([g] * (W // tile), axis=0)
            wide[k] = jnp.where(spot[0] == spot[1], g, 0.0).astype(BF)
    pl.semaphore_wait(barrier, count)

    def remote(src, dst, ss, rs, r, c):
        return pltpu.make_async_remote_copy(
            src_ref=src, dst_ref=dst, send_sem=ss, recv_sem=rs, device_id=(r, c), device_id_type=MESH)

    def to_left(i):
        return remote(chunk(y_hbm, i), chunk(yr, i), yr_s.at[i], yr_r.at[i], n, l - 1)

    def to_down(i):
        return remote(chunk(y_hbm, i), chunk(yd, i), yd_s.at[i], yd_r.at[i], n - 1, l)

    def z_up(i):
        return remote(zt.at[i], zin.at[i], z_s.at[i], z_r.at[i], n + 1, l)

    gv_left = lambda: remote(bdv.at[1], bdvr, g_s.at[0], g_r.at[0], n, l - 1)
    go_down = lambda: remote(bdo.at[1], bdor, g_s.at[1], g_r.at[1], n - 1, l)

    def cut(ref, i, k):
        at, size = parts[k]
        return ref.at[pl.ds(i * C, C), pl.ds(at, size)]

    def part_direct(i):
        return remote(cut(y_hbm, i, 0), cut(yr, i, 0), part_s.at[i, 0], part_r.at[i, 0], n, l - 1)

    def part_out(i, k):
        return remote(cut(y_hbm, i, k), rel.at[i, :, pl.ds(0, parts[k][1])], part_s.at[i, k], rel_r.at[i], n, half + 2 * k)

    def part_on(i, k):
        return remote(rel.at[i, :, pl.ds(0, parts[k][1])], cut(yr, i, k), rel_s.at[i], part_r.at[i, k], n, half - 1)

    @pl.when(has_left)
    def _():
        gv_left().start()

    @pl.when(is_src)
    def _():
        for i in range(nch):
            part_direct(i).start()
            for k in through:
                part_out(i, k).start()

    @pl.when(has_left & jnp.logical_not(is_src))
    def _():
        for i in range(nch):
            to_left(i).start()

    def side_y(ref, i, h):
        return ref.at[pl.ds(i * C, C), pl.ds(h * (width // 2), width // 2)]

    def side_z(ref, i, h):
        return ref.at[i, pl.ds(h * (width // 2), width // 2), :]

    def yw_direct(i):
        return remote(side_y(y_hbm, i, 0), side_y(yd, i, 0), yw_s.at[i, 0], yw_r.at[i, 0], n - 1, l)

    def yw_out(i):
        return remote(side_y(y_hbm, i, 1), rely.at[i], yw_s.at[i, 1], ry_r.at[i], n + nx - 1, l - 1)

    def yw_on(i):
        return remote(rely.at[i], side_y(yd, i, 1), ry_s.at[i], yw_r.at[i, 1], n - nx, l + 1)

    def zw_direct(i):
        return remote(side_z(zt, i, 0), side_z(zin, i, 0), zw_s.at[i, 0], zw_r.at[i, 0], n + 1, l)

    def zw_out(i):
        return remote(side_z(zt, i, 1), relz.at[i], zw_s.at[i, 1], rz_r.at[i], n - nx + 1, l)

    def zw_on(i):
        return remote(relz.at[i], side_z(zin, i, 1), rz_s.at[i], zw_r.at[i, 1], n + nx, l)

    plain_y = has_dn & odd & jnp.logical_not(lead)
    plain_z = has_up & even & jnp.logical_not(tail)

    @pl.when(has_dn & odd)
    def _():
        go_down().start()

    @pl.when(src_y)
    def _():
        for i in range(nch):
            yw_direct(i).start()
            yw_out(i).start()

    @pl.when(plain_y)
    def _():
        for i in range(nch):
            to_down(i).start()

    for i in range(nch):
        local(i).wait()

    def spread(g):
        return jnp.concatenate(
            [t32[pl.ds(g * (W // tile) + j, tile, stride=tile), :] for j in range(W // tile)], axis=0)

    def make_z(i, right):
        def one(b, _):
            at = pl.ds(b * W, W)
            z = dot_nt(bdv[0], y[pl.ds(i * C, C), at])
            if right:
                z = z + dot_nt(bdvr[...], yr[pl.ds(i * C, C), at])
            t32[at, :] = z
            return 0
        lax.fori_loop(0, nblk, one, 0, unroll=True)

        def two(g, _):
            zt[i, pl.ds(g * W, W), :] = spread(g).astype(BF)
            return 0
        lax.fori_loop(0, nblk, two, 0, unroll=True)

    def make_x(src, i, targets):
        def one(b, _):
            at = pl.ds(b * W, W)
            t32[at, :] = jnp.transpose(src[pl.ds(i * C, C), at].astype(F32))
            return 0
        lax.fori_loop(0, nblk, one, 0, unroll=True)

        def two(g, _):
            part = jnp.transpose(spread(g)).astype(BF)
            for green, dst in targets:
                dst[pl.ds(i * C, C), pl.ds(g * W, W)] = dot_nn(part, green()).astype(BF)
            return 0
        lax.fori_loop(0, nblk, two, 0, unroll=True)

    def chi_cols(acc, i, x, z):
        acc[i] = jnp.zeros((aux, C), F32)

        def one(k, _):
            at = pl.ds(k * STEP, STEP)
            acc[i] += dot_nn(x[:, at], z[i, at, :])
            return 0
        lax.fori_loop(0, width // STEP, one, 0)

    def chi_tile(acc, p, q, x, z):
        at_p = pl.ds(p * C, C)
        acc[q, at_p, :] = dot_nn(x[at_p, :], z[q])

    def fill(acc, s0, i):
        for d in range(cols):
            s0[i, d % 2, d // 2] = acc[i, d * own:(d + 1) * own, :].astype(BF)

    def d0(i):
        return remote(s0d.at[i, 1 - core], r0d.at[i], d0_s.at[i], d0_r.at[i], n, l + 1 - 2 * core)

    def n0_even(i, c):
        return remote(s0n.at[i, c], r0n.at[i, 0], n0_s.at[i, c], n0_r.at[i, 0], n - 1, l + c)

    def n0_odd(i):
        return remote(s0n.at[i, 0], r0n.at[i, 1], n0_s.at[i, 0], n0_r.at[i, 1], n, l - 1)

    def scatter_d(i):
        fill(accd, s0d, i)
        d0(i).start()

    def scatter_n_even(i):
        fill(accn, s0n, i)
        n0_even(i, 0).start()
        n0_even(i, 1).start()

    def scatter_n_odd(i):
        fill(accn, s0n, i)
        n0_odd(i).start()

    def a_copy(sa, ra, ss, rs, i, k):
        to = lax.rem(iy + k, ny)
        return remote(sa.at[i, to], ra.at[i, iy], ss.at[i, to], rs.at[i, iy], n, y_peer(k))

    def a_send(first, second, sa, ra, ss, rs, i):
        for z in range(2):
            for k in range(ny):
                at = z * ny + k
                sa[i, k, z] = (first(at).astype(F32) + second(at).astype(F32)).astype(BF)
        ra[i, iy] = sa[i, iy]
        for k in range(1, ny):
            a_copy(sa, ra, ss, rs, i, k).start()

    def a_d(i):
        d0(i).wait_recv()
        a_send(lambda at: s0d[i, core, at], lambda at: r0d[i, at], sad, rad, da_s, da_r, i)

    def a_n(i):
        n0_even(i, 0).wait_recv()

        @pl.when(even)
        def _():
            n0_odd(i).wait_recv()
            a_send(lambda at: r0n[i, 0, at], lambda at: r0n[i, 1, at], san, ran, na_s, na_r, i)

        @pl.when(odd)
        def _():
            a_send(lambda at: r0n[i, 0, at], lambda at: s0n[i, 1, at], san, ran, na_s, na_r, i)

    def b_copy(sb, rb, ss, rs, i):
        return remote(sb.at[i], rb.at[i], ss.at[i], rs.at[i], n, z_peer)

    def b_send(sa, ra, sas, sar, sb, rb, ss, rs, out, i):
        for k in range(1, ny):
            j = lax.rem(iy + k, ny)
            remote(sa.at[i, j], ra.at[i, j], sas.at[i, j], sar.at[i, j], n, l).wait_recv()

        def total(z):
            t = ra[i, 0, z].astype(F32)
            for j in range(1, ny):
                t = t + ra[i, j, z].astype(F32)
            return t
        sb[i] = total(1 - iz).astype(BF)
        b_copy(sb, rb, ss, rs, i).start()
        out[:, pl.ds(pl.multiple_of(i * C, C), C)] = total(iz)

    def b_d(i):
        b_send(sad, rad, da_s, da_r, sbd, rbd, db_s, db_r, outd, i)

    def b_n(i):
        b_send(san, ran, na_s, na_r, sbn, rbn, nb_s, nb_r, outn, i)

    def last(sb, rb, ss, rs, out, i):
        b_copy(sb, rb, ss, rs, i).wait_recv()
        out[:, pl.ds(pl.multiple_of(i * C, C), C)] += rb[i].astype(F32)

    def settle(i):
        @pl.when(i >= 1)
        def _():
            a_d(i - 1)

        @pl.when(i == nch - 1)
        def _():
            lax.fori_loop(0, nch - 2, lambda k, c: (b_d(k), c)[1], 0)

    def each(f):
        def g(i, _):
            f(i)
            return 0
        lax.fori_loop(0, nch, g, 0)

    def right_chunk(i):
        return remote(chunk(y_hbm, i), chunk(yr, i), yr_s.at[i], yr_r.at[i], n, l)

    @pl.when(even)
    def _():
        remote(bdv.at[1], bdvr, g_s.at[0], g_r.at[0], n, l).wait_recv()

        def first(i):
            right_chunk(i).wait_recv()
            make_z(i, True)

            @pl.when(plain_z)
            def _():
                z_up(i).start()

            @pl.when(src_z)
            def _():
                zw_direct(i).start()
                zw_out(i).start()

            for k in through:
                @pl.when(l == half + 2 * k)
                def _():
                    part_out(i, k).wait_recv()
                    part_on(i, k).start()
        each(first)

        def pass_on(i):
            @pl.when(rel_y)
            def _():
                yw_out(i).wait_recv()
                yw_on(i).start()

            @pl.when(rel_z)
            def _():
                zw_out(i).wait_recv()
                zw_on(i).start()

        def halves(i):
            make_x(y, i, ((lambda: bdo[0], xa), (lambda: bdo[1], xb)))
            for at, k in ((2, 0), (4, 1)):
                @pl.when(i == min(at, nch - 1))
                def _():
                    if k < nch:
                        pass_on(k)
        each(halves)

        def second(i):
            chi_cols(accd, i, xa, zt)
            scatter_d(i)
            for at, k in ((1, 2), (4, 3)):
                @pl.when(i == min(at, nch - 1))
                def _():
                    if k < nch:
                        pass_on(k)
        each(second)

        def third(i):
            settle(i)

            @pl.when(has_dn)
            def _():
                @pl.when(lead)
                def _():
                    zw_direct(i).wait_recv()
                    zw_on(i).wait_recv()

                @pl.when(jnp.logical_not(lead))
                def _():
                    remote(zt.at[i], zin.at[i], z_s.at[i], z_r.at[i], n, l).wait_recv()
                chi_cols(accn, i, xb, zin)
                scatter_n_even(i)

            if nch > 4:
                @pl.when(i == 3)
                def _():
                    pass_on(4)
        each(third)

    @pl.when(odd)
    def _():
        each(lambda i: make_x(y, i, ((lambda: bdo[0], xa),)))

        @pl.when(has_right)
        def _():
            remote(bdv.at[1], bdvr, g_s.at[0], g_r.at[0], n, l).wait_recv()

        @pl.when(has_up)
        def _():
            remote(bdo.at[1], bdor, g_s.at[1], g_r.at[1], n, l).wait_recv()

        def step(i):
            @pl.when(has_right)
            def _():
                @pl.when(is_dst)
                def _():
                    for k in parts:
                        remote(cut(y_hbm, i, k), cut(yr, i, k), part_s.at[i, k], part_r.at[i, k], n, l).wait_recv()

                @pl.when(jnp.logical_not(is_dst))
                def _():
                    right_chunk(i).wait_recv()
                make_z(i, True)

            @pl.when(jnp.logical_not(has_right))
            def _():
                make_z(i, False)
            chi_cols(accd, i, xa, zt)
            scatter_d(i)

            @pl.when(has_up)
            def _():
                def a(p, _):
                    chi_tile(accn, p, i, xb, zt)
                    return 0
                lax.fori_loop(0, i, a, 0)

            settle(i)

            @pl.when(has_up)
            def _():
                @pl.when(tail)
                def _():
                    yw_direct(i).wait_recv()
                    yw_on(i).wait_recv()

                @pl.when(jnp.logical_not(tail))
                def _():
                    remote(chunk(y_hbm, i), chunk(yd, i), yd_s.at[i], yd_r.at[i], n, l).wait_recv()
                make_x(yd, i, ((lambda: bdor[...], xb),))

                def b(q, _):
                    chi_tile(accn, i, q, xb, zt)

                    @pl.when(i == nch - 1)
                    def _():
                        scatter_n_odd(q)
                    return 0
                lax.fori_loop(0, i + 1, b, 0)
        each(step)

    a_d(nch - 1)

    @pl.when(has_up)
    def _():
        each(a_n)
    b_d(nch - 2)
    b_d(nch - 1)

    @pl.when(has_up)
    def _():
        each(b_n)
    each(lambda i: last(sbd, rbd, db_s, db_r, outd, i))

    @pl.when(has_up)
    def _():
        each(lambda i: last(sbn, rbn, nb_s, nb_r, outn, i))

    @pl.when(jnp.logical_not(has_up))
    def _():
        outn[...] = jnp.zeros_like(outn)

    @pl.when(has_left)
    def _():
        gv_left().wait_send()

    @pl.when(is_src)
    def _():
        for i in range(nch):
            part_direct(i).wait_send()
            for k in through:
                part_out(i, k).wait_send()

    for k in through:
        @pl.when(l == half + 2 * k)
        def _():
            for i in range(nch):
                part_on(i, k).wait_send()

    @pl.when(has_left & jnp.logical_not(is_src))
    def _():
        for i in range(nch):
            to_left(i).wait_send()

    @pl.when(has_dn & odd)
    def _():
        go_down().wait_send()

    @pl.when(plain_y)
    def _():
        for i in range(nch):
            to_down(i).wait_send()

    @pl.when(plain_z)
    def _():
        for i in range(nch):
            z_up(i).wait_send()

    @pl.when(src_y)
    def _():
        for i in range(nch):
            yw_direct(i).wait_send()
            yw_out(i).wait_send()

    @pl.when(src_z)
    def _():
        for i in range(nch):
            zw_direct(i).wait_send()
            zw_out(i).wait_send()

    @pl.when(rel_y)
    def _():
        for i in range(nch):
            yw_on(i).wait_send()

    @pl.when(rel_z)
    def _():
        for i in range(nch):
            zw_on(i).wait_send()

    def sent_d(i):
        d0(i).wait_send()
        b_copy(sbd, rbd, db_s, db_r, i).wait_send()
        for k in range(1, ny):
            a_copy(sad, rad, da_s, da_r, i, k).wait_send()
    each(sent_d)

    @pl.when(has_up)
    def _():
        def sent_n(i):
            b_copy(sbn, rbn, nb_s, nb_r, i).wait_send()
            for k in range(1, ny):
                a_copy(san, ran, na_s, na_r, i, k).wait_send()
        each(sent_n)

    @pl.when(has_dn & even)
    def _():
        each(lambda i: (n0_even(i, 0).wait_send(), n0_even(i, 1).wait_send()))

    @pl.when(has_up & odd)
    def _():
        each(lambda i: n0_odd(i).wait_send())


def solution(mesh):
    rows, cols = mesh.shape["row"], mesh.shape["col"]

    def body(three_centre, green_occ, green_vir, pair_live):
        aux, width = three_centre.shape[2:]
        tile = green_occ.shape[2]
        nch, own = aux // C, aux // cols
        half = cols // 2
        ny = half // 2
        nx = math.isqrt(rows)
        dma = pltpu.SemaphoreType.DMA
        vm = lambda *s: pltpu.VMEM(s, BF)
        out = pl.pallas_call(
            functools.partial(kernel, rows, cols, nx, tile),
            out_shape=jax.ShapeDtypeStruct((2, own, aux), F32),
            in_specs=[
                pl.BlockSpec(memory_space=pl.ANY),
                pl.BlockSpec(memory_space=pltpu.VMEM),
                pl.BlockSpec(memory_space=pltpu.VMEM),
                pl.BlockSpec(memory_space=pltpu.SMEM),
            ],
            out_specs=pl.BlockSpec(memory_space=pltpu.VMEM),
            scratch_shapes=[
                vm(2, W, W), vm(2, W, W),
                vm(aux, width), vm(aux, width), vm(aux, width),
                vm(nch, width, C), vm(nch, width, C),
                vm(aux, width), vm(aux, width),
                pltpu.VMEM((width, C), F32),
                pltpu.VMEM((nch, aux, C), F32), pltpu.VMEM((nch, aux, C), F32),
                vm(W, W), vm(W, W), vm(nch, C, max(size for _, size in shares(width, ny).values())), vm(nch, C, width // 2), vm(nch, width // 2, C),
                vm(nch, 2, half, own, C), vm(nch, 2, half, own, C), vm(nch, half, own, C), vm(nch, 2, half, own, C),
                vm(nch, ny, 2, own, C), vm(nch, ny, 2, own, C), vm(nch, ny, 2, own, C), vm(nch, ny, 2, own, C),
                vm(nch, own, C), vm(nch, own, C), vm(nch, own, C), vm(nch, own, C),
                *[dma((nch,))] * 7,
                dma((2,)), dma((2,)), dma((nch,)), dma((nch,)), dma((nch, ny)), dma((nch, ny)),
                dma((nch,)), dma((nch,)), dma((nch, 2)), dma((nch, 2)), dma((nch,)), dma((nch,)), dma((nch, 2)), dma((nch, 2)),
                dma((nch,)), dma((nch,)), dma((nch, 2)), dma((nch, 2)),
                *[dma((nch, ny))] * 4, *[dma((nch,))] * 4,
            ],
            compiler_params=pltpu.CompilerParams(
                collective_id=0, has_side_effects=True, vmem_limit_bytes=60 * 1024 * 1024),
        )(three_centre[0, 0], green_occ[0], green_vir[0], pair_live)
        return out[0][None], out[1][None]

    return jax.shard_map(
        body,
        mesh=mesh,
        in_specs=(
            P("row", "col", None, None),
            P("row", None, None, None),
            P("col", None, None, None),
            P("row", "col"),
        ),
        out_specs=(P("row", "col", None), P("row", "col", None)),
        check_vma=False,
    )
```
